128 devices in a mesh: inp: 8 (over x_lo, z), tm: 16 (over x_hi, y, core).
Axes of the slice: x: 4 (x_hi: 2, x_lo: 2; x = x_hi * 2 + x_lo), y: 4, z: 4, core: 2. Of those that a mesh axis runs over, the one named last changes fastest.
Arguments:
- samples: bfloat16 [512, 1024, 1024], P('inp', 'tm'), may hold values from -6 to 6
- eq_gain: float32 [512, 512], P(None, 'inp'), may hold values from 0.5 to 2
Outputs:
- visibilities: float32 [512, 2, 512, 512], P(('inp', 'tm'))
The draws below stay inside these ranges and needn't reach their ends.
All inputs are finite; a program needn't handle non-finite values.
Results may differ from the reference program's by a relative error of at most 0.0033.
Values may be sent and summed in bfloat16 or wider, within the bound.
No kernel may reach another device: no remote copies, remote signals or barrier semaphores. Data moves between devices by JAX's collectives and lax.ppermute only.
A program may use at most 192 MiB of HBM per device.

```python
import math
import jax
import jax.numpy as jnp
from jax import lax

INPUTS = 512
CHANNELS = 512
TAPS = 4
NFFT = 1024
FRAMES = 1024


def shard_levels(key, shape, pieces, low, high):
    def one(axis_at, shards_of):
        draws = jax.random.uniform(jax.random.fold_in(jax.random.fold_in(key, 6), axis_at), (shards_of,), jnp.float32, low / len(pieces), high / len(pieces))
        return jnp.repeat(jnp.exp(draws), shape[axis_at] // shards_of).reshape((-1,) + (1,) * (len(shape) - axis_at - 1))

    loudness = one(*pieces[0])
    for cut in pieces[1:]:
        loudness = loudness * one(*cut)
    return loudness


def normal_values(rng, dims, width, most, split=(), kind=jnp.bfloat16):
    values = jax.random.normal(rng, dims, jnp.float32) * width
    if len(split) > 0:
        values = shard_levels(rng, dims, split, -0.22, 0.18) * values
    return jnp.clip(values, min=-most, max=most).astype(kind)


def setup_inputs(seed: int = 0) -> dict:
    arg_keys = jax.random.split(jax.random.key(seed), 3)
    return {
        "samples": normal_values(arg_keys[0], (INPUTS, FRAMES, NFFT), 1.0, 6.0, ((0, 8), (1, 16))),
        "eq_gain": jnp.clip(jnp.exp(math.log(2.0) - 1.3862944 * jax.random.uniform(arg_keys[1], (CHANNELS, INPUTS), jnp.float32) ** shard_levels(arg_keys[1], (CHANNELS, INPUTS), ((1, 8),), -0.2, 0.2)), 0.5, 2.0),
    }


def window_table(taps, nfft):
    position = jnp.arange(taps * nfft, dtype=jnp.int32).astype(jnp.float32) + 0.5
    shape_part = jnp.sinc(position / nfft - taps / 2.0)
    taper = 0.5 - 0.5 * jnp.cos(position * (2.0 * math.pi / (taps * nfft)))
    return (shape_part * taper).reshape(taps, nfft)

def fourier_table(channels, nfft):
    chan = jnp.arange(channels, dtype=jnp.int32)
    point = jnp.arange(nfft, dtype=jnp.int32)
    phase = (chan[:, None] * point[None, :] % nfft).astype(jnp.float32) * (2.0 * math.pi / nfft)
    scale = 1.0 / math.sqrt(nfft)
    table = jnp.stack([jnp.cos(phase) * scale, -jnp.sin(phase) * scale], axis=1)
    return table.reshape(2 * channels, nfft).astype(jnp.bfloat16)

def reference(samples, eq_gain):
    frames_all = samples.shape[1]
    nfft = samples.shape[2]
    channels = nfft // 2
    window = window_table(TAPS, nfft)
    table = fourier_table(channels, nfft)
    block = min(64, INPUTS)
    grouped = samples.reshape(INPUTS // block, block, frames_all, nfft)
    gains = eq_gain.T.reshape(INPUTS // block, block, channels)

    def channelize(pair):
        piece, gain = pair
        padded = jnp.concatenate([jnp.zeros((block, TAPS - 1, nfft), jnp.bfloat16), piece], axis=1)
        filtered = jnp.zeros((block, frames_all, nfft), jnp.float32)
        for tap in range(TAPS):
            filtered = filtered + window[tap] * padded[:, tap:tap + frames_all, :].astype(jnp.float32)
        filtered = filtered.astype(jnp.bfloat16)
        rows = filtered.reshape(block * frames_all, nfft)
        spectra = jnp.dot(rows, table.T, preferred_element_type=jnp.float32)
        spectra = spectra.reshape(block, frames_all, channels, 2) * gain[:, None, :, None]
        return spectra.astype(jnp.bfloat16)
    spectra = lax.map(channelize, (grouped, gains))
    spectra = spectra.reshape(INPUTS, frames_all, channels, 2).transpose(2, 3, 0, 1)

    def correlate(single):
        stacked = single.reshape(2 * INPUTS, frames_all)
        gram = jnp.dot(stacked, stacked.T, preferred_element_type=jnp.float32)
        real_part = (gram[:INPUTS, :INPUTS] + gram[INPUTS:, INPUTS:]) / frames_all
        imag_part = (gram[INPUTS:, :INPUTS] - gram[:INPUTS, INPUTS:]) / frames_all
        return jnp.stack([real_part, imag_part])
    return lax.map(correlate, spectra)
```

```python
import functools
import math

import jax
import jax.numpy as jnp
import ml_dtypes
import numpy as np
from jax import lax
from jax.experimental import pallas as pl
from jax.experimental.pallas import tpu as pltpu
from jax.sharding import PartitionSpec as P

TAPS = 4
CHUNKS = 2
BLOCK = 16
SUB = 4


def passed_along(array, axis, by):
    devices = lax.axis_size(axis)
    pairs = [(i, i + by) for i in range(devices) if 0 <= i + by < devices]
    return lax.ppermute(array, axis, pairs)


def window_table(taps, nfft):
    position = np.arange(taps * nfft, dtype=np.float64) + 0.5
    shape_part = np.sinc(position / nfft - taps / 2.0)
    taper = 0.5 - 0.5 * np.cos(position * (2.0 * math.pi / (taps * nfft)))
    return (shape_part * taper).reshape(taps, nfft).astype(np.float32)


def fourier_tables(channels, nfft, groups):
    chan = np.arange(channels)
    phase = (chan[:, None] * np.arange(nfft)[None, :] % nfft) * (2.0 * math.pi / nfft)
    scale = 1.0 / math.sqrt(nfft)
    table = np.stack([np.cos(phase) * scale, -np.sin(phase) * scale])
    table = table.astype(np.float32).astype(ml_dtypes.bfloat16)
    each = channels // groups // CHUNKS
    table = table.reshape(2, groups, CHUNKS, each, nfft).transpose(2, 0, 1, 3, 4)
    return table.reshape(CHUNKS, 2 * groups * each, nfft)


def channelize_kernel(table_ref, gain_ref, rows_ref, out_ref, turned):
    inputs, frames, nfft = rows_ref.shape
    count = table_ref.shape[0] // 2
    table = table_ref[...]
    lane = lax.broadcasted_iota(jnp.int32, (count, 2 * frames), 1)
    first = lane < frames
    for s in range(inputs // SUB):
        rows = rows_ref[s * SUB : (s + 1) * SUB].reshape(SUB * frames, nfft)
        both = lax.dot_general(
            table, rows, (((1,), (1,)), ((), ())), preferred_element_type=jnp.float32
        )
        for j in range(SUB // 2):
            real = both[:count, j * 2 * frames : (j + 1) * 2 * frames]
            imag = both[count:, j * 2 * frames : (j + 1) * 2 * frames]
            even = jnp.where(first, real, pltpu.roll(imag, frames, 1))
            odd = jnp.where(first, pltpu.roll(real, frames, 1), imag)
            a = s * SUB + 2 * j
            turned[pl.ds(a, count, stride=inputs), :] = even * gain_ref[0, :, a : a + 1]
            turned[pl.ds(a + 1, count, stride=inputs), :] = odd * gain_ref[0, :, a + 1 : a + 2]
    out_ref[...] = turned[...].reshape(count, inputs, 2 * frames).astype(out_ref.dtype)


def channelize(table, gain, filtered):
    inputs, frames, nfft = filtered.shape
    count = table.shape[0] // 2
    return pl.pallas_call(
        channelize_kernel,
        grid=(inputs // BLOCK,),
        in_specs=[
            pl.BlockSpec(table.shape, lambda i: (0, 0)),
            pl.BlockSpec((1, count, BLOCK), lambda i: (i, 0, 0)),
            pl.BlockSpec((BLOCK, frames, nfft), lambda i: (i, 0, 0)),
        ],
        out_specs=pl.BlockSpec((count, BLOCK, 2 * frames), lambda i: (0, i, 0)),
        out_shape=jax.ShapeDtypeStruct((count, inputs, 2 * frames), jnp.bfloat16),
        scratch_shapes=[pltpu.VMEM((count * BLOCK, 2 * frames), jnp.float32)],
        compiler_params=pltpu.CompilerParams(
            dimension_semantics=("arbitrary",), vmem_limit_bytes=40 * 2**20
        ),
        cost_estimate=pl.CostEstimate(
            flops=4 * count * inputs * frames * nfft,
            transcendentals=0,
            bytes_accessed=2 * (inputs * frames * nfft + count * inputs * 2 * frames),
        ),
        name="channelize",
    )(table, gain, filtered)


def correlate_kernel(frames_all, blocks_ref, *refs):
    out_ref = refs[-1]
    n_time = blocks_ref.shape[1]
    inputs_all = blocks_ref.shape[0] * blocks_ref.shape[3]
    width = blocks_ref.shape[4]
    half = width // 2
    straight, crossed = [], []
    for t in range(n_time):
        part = blocks_ref[:, t, 0].reshape(inputs_all, width)
        straight.append(part)
        crossed.append(jnp.concatenate([part[:, half:], -part[:, :half]], axis=1))
    straight = jnp.concatenate(straight, axis=1)
    crossed = jnp.concatenate(crossed, axis=1)
    last = (((1,), (1,)), ((), ()))
    scale = 1.0 / frames_all
    out_ref[0, 0] = (
        lax.dot_general(straight, straight, last, preferred_element_type=jnp.float32) * scale
    )
    out_ref[0, 1] = (
        lax.dot_general(crossed, straight, last, preferred_element_type=jnp.float32) * scale
    )


def correlate(arrived, before, chunk, chan_dev, frames_all):
    n_inp, n_time, each, local, width = arrived.shape
    inputs_all = n_inp * local
    operands = [arrived]
    in_specs = [pl.BlockSpec((n_inp, n_time, 1, local, width), lambda i: (0, 0, i, 0, 0))]
    aliases = {}
    if before is not None:
        operands.append(before)
        in_specs.append(pl.BlockSpec(memory_space=pl.ANY))
        aliases = {1: 0}
    return pl.pallas_call(
        functools.partial(correlate_kernel, frames_all),
        grid=(each,),
        in_specs=in_specs,
        out_specs=pl.BlockSpec(
            (1, 2, inputs_all, inputs_all), lambda i: (chunk * each + i, 0, 0, 0)
        ),
        out_shape=jax.ShapeDtypeStruct((chan_dev, 2, inputs_all, inputs_all), jnp.float32),
        input_output_aliases=aliases,
        compiler_params=pltpu.CompilerParams(
            dimension_semantics=("arbitrary",), vmem_limit_bytes=40 * 2**20
        ),
        cost_estimate=pl.CostEstimate(
            flops=each * 4 * inputs_all * inputs_all * n_time * width,
            transcendentals=0,
            bytes_accessed=each * (2 * inputs_all * n_time * width + 8 * inputs_all * inputs_all),
        ),
        name="correlate",
    )(*operands)


def on_device(samples, eq_gain):
    local_inputs, local_frames, nfft = samples.shape
    channels = nfft // 2
    n_inp = lax.axis_size("inp")
    n_time = lax.axis_size("tm")
    groups = n_inp * n_time
    chan_dev = channels // groups
    each = chan_dev // CHUNKS
    frames_all = n_time * local_frames
    tail = samples[:, local_frames - (TAPS - 1) :, :]
    before = passed_along(tail, "tm", 1)
    padded = jnp.concatenate([before, samples], axis=1)
    window = window_table(TAPS, nfft)
    filtered = jnp.zeros((local_inputs, local_frames, nfft), jnp.float32)
    for tap in range(TAPS):
        filtered = filtered + window[tap] * padded[:, tap : tap + local_frames, :].astype(
            jnp.float32
        )
    filtered = filtered.astype(jnp.bfloat16)
    tables = fourier_tables(channels, nfft, groups)
    gains = eq_gain.reshape(groups, CHUNKS, each, local_inputs // BLOCK, BLOCK)
    gains = gains.transpose(1, 3, 0, 2, 4).reshape(
        CHUNKS, local_inputs // BLOCK, groups * each, BLOCK
    )
    visibilities = None
    for k in range(CHUNKS):
        parcel = channelize(jnp.asarray(tables[k]), gains[k], filtered)
        parcel = parcel.reshape(groups, each * local_inputs, 2 * local_frames)
        arrived = lax.all_to_all(
            parcel, ("inp", "tm"), split_axis=0, concat_axis=0, tiled=True
        )
        arrived = arrived.reshape(n_inp, n_time, each, local_inputs, 2 * local_frames)
        visibilities = correlate(arrived, visibilities, k, chan_dev, frames_all)
    return visibilities


def solution(mesh):
    placed = (P("inp", "tm", None), P(None, "inp"))
    return jax.shard_map(
        on_device,
        mesh=mesh,
        in_specs=placed,
        out_specs=P(("inp", "tm"), None, None, None),
        check_vma=False,
    )
```

```python
import functools
import math

import jax
import jax.numpy as jnp
import ml_dtypes
import numpy as np
from jax import lax
from jax.experimental import pallas as pl
from jax.experimental.pallas import tpu as pltpu
from jax.sharding import PartitionSpec as P

TAPS = 4
CHUNKS = 2
BLOCK = 16
LANES = 128
SUB = 4


def passed_along(array, axis, by):
    devices = lax.axis_size(axis)
    pairs = [(i, i + by) for i in range(devices) if 0 <= i + by < devices]
    return lax.ppermute(array, axis, pairs)


def window_table(taps, nfft):
    position = np.arange(taps * nfft, dtype=np.float64) + 0.5
    shape_part = np.sinc(position / nfft - taps / 2.0)
    taper = 0.5 - 0.5 * np.cos(position * (2.0 * math.pi / (taps * nfft)))
    return (shape_part * taper).reshape(taps, nfft).astype(np.float32)


def fourier_tables(channels, nfft, groups):
    chan = np.arange(channels)
    phase = (chan[:, None] * np.arange(nfft)[None, :] % nfft) * (2.0 * math.pi / nfft)
    scale = 1.0 / math.sqrt(nfft)
    table = np.stack([np.cos(phase) * scale, -np.sin(phase) * scale])
    table = table.astype(np.float32).astype(ml_dtypes.bfloat16)
    each = channels // groups // CHUNKS
    table = table.reshape(2, groups, CHUNKS, each, nfft).transpose(2, 0, 1, 3, 4)
    return table.reshape(CHUNKS, 2 * groups * each, nfft)


def filtered_rows(samples_ref, halo_ref, window, a):
    nfft = samples_ref.shape[2]
    columns = []
    for start in range(0, nfft, LANES):
        lanes = slice(start, start + LANES)
        earlier = halo_ref[a, :, lanes].astype(jnp.float32)
        unused = jnp.zeros((8 - earlier.shape[0], LANES), jnp.float32)
        frames = samples_ref[a, :, lanes].astype(jnp.float32)
        frames = jnp.concatenate([unused, earlier, frames], axis=0)
        total = frames * window[0][:, lanes]
        for tap in range(1, TAPS):
            total = pltpu.roll(total, 1, 0) + frames * window[tap][:, lanes]
        columns.append(total[8:].astype(jnp.bfloat16))
    return jnp.concatenate(columns, axis=1)


def channelize_kernel(table_ref, gain_ref, window_ref, halo_ref, samples_ref, out_ref, turned):
    inputs, frames, nfft = samples_ref.shape
    count = table_ref.shape[0] // 2
    table = table_ref[...]
    window = [window_ref[tap : tap + 1, :] for tap in range(TAPS)]
    lane = lax.broadcasted_iota(jnp.int32, (count, 2 * frames), 1)
    first = lane < frames
    for s in range(inputs // SUB):
        rows = jnp.concatenate(
            [
                filtered_rows(samples_ref, halo_ref, window, a)
                for a in range(s * SUB, (s + 1) * SUB)
            ],
            axis=0,
        )
        both = lax.dot_general(
            table, rows, (((1,), (1,)), ((), ())), preferred_element_type=jnp.float32
        )
        for j in range(SUB // 2):
            real = both[:count, j * 2 * frames : (j + 1) * 2 * frames]
            imag = both[count:, j * 2 * frames : (j + 1) * 2 * frames]
            even = jnp.where(first, real, pltpu.roll(imag, frames, 1))
            odd = jnp.where(first, pltpu.roll(real, frames, 1), imag)
            a = s * SUB + 2 * j
            turned[pl.ds(a, count, stride=inputs), :] = even * gain_ref[0, :, a : a + 1]
            turned[pl.ds(a + 1, count, stride=inputs), :] = odd * gain_ref[0, :, a + 1 : a + 2]
    out_ref[...] = turned[...].reshape(count, inputs, 2 * frames).astype(out_ref.dtype)


def channelize(table, gain, window, halo, samples):
    inputs, frames, nfft = samples.shape
    count = table.shape[0] // 2
    return pl.pallas_call(
        channelize_kernel,
        grid=(inputs // BLOCK,),
        in_specs=[
            pl.BlockSpec(table.shape, lambda i: (0, 0)),
            pl.BlockSpec((1, count, BLOCK), lambda i: (i, 0, 0)),
            pl.BlockSpec(window.shape, lambda i: (0, 0)),
            pl.BlockSpec((BLOCK, TAPS - 1, nfft), lambda i: (i, 0, 0)),
            pl.BlockSpec((BLOCK, frames, nfft), lambda i: (i, 0, 0)),
        ],
        out_specs=pl.BlockSpec((count, BLOCK, 2 * frames), lambda i: (0, i, 0)),
        out_shape=pltpu.HBM((count, inputs, 2 * frames), jnp.bfloat16),
        scratch_shapes=[pltpu.VMEM((count * BLOCK, 2 * frames), jnp.float32)],
        compiler_params=pltpu.CompilerParams(
            dimension_semantics=("arbitrary",), vmem_limit_bytes=40 * 2**20
        ),
        cost_estimate=pl.CostEstimate(
            flops=4 * count * inputs * frames * nfft,
            transcendentals=0,
            bytes_accessed=2 * (inputs * frames * nfft + count * inputs * 2 * frames),
        ),
        name="channelize",
    )(table, gain, window, halo, pltpu.with_memory_space_constraint(samples, pltpu.HBM))


def correlate_kernel(frames_all, blocks_ref, *refs):
    out_ref = refs[-1]
    n_time = blocks_ref.shape[1]
    inputs_all = blocks_ref.shape[0] * blocks_ref.shape[3]
    width = blocks_ref.shape[4]
    half = width // 2
    straight, crossed = [], []
    for t in range(n_time):
        part = blocks_ref[:, t, 0].reshape(inputs_all, width)
        straight.append(part)
        crossed.append(jnp.concatenate([part[:, half:], -part[:, :half]], axis=1))
    straight = jnp.concatenate(straight, axis=1)
    crossed = jnp.concatenate(crossed, axis=1)
    last = (((1,), (1,)), ((), ()))
    scale = 1.0 / frames_all
    out_ref[0, 0] = (
        lax.dot_general(straight, straight, last, preferred_element_type=jnp.float32) * scale
    )
    out_ref[0, 1] = (
        lax.dot_general(crossed, straight, last, preferred_element_type=jnp.float32) * scale
    )


def correlate(arrived, before, chunk, chan_dev, frames_all):
    n_inp, n_time, each, local, width = arrived.shape
    inputs_all = n_inp * local
    operands = [arrived]
    in_specs = [pl.BlockSpec((n_inp, n_time, 1, local, width), lambda i: (0, 0, i, 0, 0))]
    aliases = {}
    if before is not None:
        operands.append(before)
        in_specs.append(pl.BlockSpec(memory_space=pl.ANY))
        aliases = {1: 0}
    return pl.pallas_call(
        functools.partial(correlate_kernel, frames_all),
        grid=(each,),
        in_specs=in_specs,
        out_specs=pl.BlockSpec(
            (1, 2, inputs_all, inputs_all), lambda i: (chunk * each + i, 0, 0, 0)
        ),
        out_shape=jax.ShapeDtypeStruct((chan_dev, 2, inputs_all, inputs_all), jnp.float32),
        input_output_aliases=aliases,
        compiler_params=pltpu.CompilerParams(
            dimension_semantics=("arbitrary",), vmem_limit_bytes=40 * 2**20
        ),
        cost_estimate=pl.CostEstimate(
            flops=each * 4 * inputs_all * inputs_all * n_time * width,
            transcendentals=0,
            bytes_accessed=each * (2 * inputs_all * n_time * width + 8 * inputs_all * inputs_all),
        ),
        name="correlate",
    )(*operands)


def on_device(samples, eq_gain):
    local_inputs, local_frames, nfft = samples.shape
    channels = nfft // 2
    n_inp = lax.axis_size("inp")
    n_time = lax.axis_size("tm")
    groups = n_inp * n_time
    chan_dev = channels // groups
    each = chan_dev // CHUNKS
    frames_all = n_time * local_frames
    tail = samples[:, local_frames - (TAPS - 1) :, :]
    before = passed_along(tail, "tm", 1)
    window = jnp.asarray(window_table(TAPS, nfft))
    tables = fourier_tables(channels, nfft, groups)
    gains = eq_gain.reshape(groups, CHUNKS, each, local_inputs // BLOCK, BLOCK)
    gains = gains.transpose(1, 3, 0, 2, 4).reshape(
        CHUNKS, local_inputs // BLOCK, groups * each, BLOCK
    )
    visibilities = None
    for k in range(CHUNKS):
        parcel = channelize(jnp.asarray(tables[k]), gains[k], window, before, samples)
        parcel = parcel.reshape(groups, each * local_inputs, 2 * local_frames)
        arrived = lax.all_to_all(
            parcel, ("inp", "tm"), split_axis=0, concat_axis=0, tiled=True
        )
        arrived = arrived.reshape(n_inp, n_time, each, local_inputs, 2 * local_frames)
        visibilities = correlate(arrived, visibilities, k, chan_dev, frames_all)
    return visibilities


def solution(mesh):
    placed = (P("inp", "tm", None), P(None, "inp"))
    return jax.shard_map(
        on_device,
        mesh=mesh,
        in_specs=placed,
        out_specs=P(("inp", "tm"), None, None, None),
        check_vma=False,
    )
```

```python
import functools
import math

import jax
import jax.numpy as jnp
import ml_dtypes
import numpy as np
from jax import lax
from jax.experimental import pallas as pl
from jax.experimental.pallas import tpu as pltpu
from jax.sharding import PartitionSpec as P

TAPS = 4
LANES = 128
SUBLANES = 8
EARLY = 16
BLOCK = 16
SUB = 4
PITCH = 24
MIB = 2**20


def passed_along(array, axis, by):
    devices = lax.axis_size(axis)
    pairs = [(i, i + by) for i in range(devices) if 0 <= i + by < devices]
    return lax.ppermute(array, axis, pairs)


def window_table(taps, nfft):
    position = np.arange(taps * nfft, dtype=np.float64) + 0.5
    shape_part = np.sinc(position / nfft - taps / 2.0)
    taper = 0.5 - 0.5 * np.cos(position * (2.0 * math.pi / (taps * nfft)))
    return (shape_part * taper).reshape(taps, nfft).astype(np.float32)


def fourier_table(channels, nfft):
    phase = (np.arange(channels)[:, None] * np.arange(nfft)[None, :] % nfft) * (
        2.0 * math.pi / nfft
    )
    scale = 1.0 / math.sqrt(nfft)
    table = np.concatenate([np.cos(phase) * scale, -np.sin(phase) * scale])
    return table.astype(np.float32).astype(ml_dtypes.bfloat16)


def summed_taps(frames, window):
    earlier = pltpu.roll(frames, 2, 0)
    odd = frames * window[2] + earlier * window[0]
    return frames * window[3] + earlier * window[1] + pltpu.roll(odd, 1, 0)


def filter_late_kernel(window_ref, samples_ref, out_ref):
    inputs, frames, nfft = samples_ref.shape
    for start in range(0, nfft, LANES):
        lanes = slice(start, start + LANES)
        window = [window_ref[tap : tap + 1, lanes] for tap in range(TAPS)]
        for a in range(inputs):
            known = samples_ref[a, EARLY - SUBLANES :, lanes].astype(jnp.float32)
            total = summed_taps(known, window)
            out_ref[a, :, lanes] = total[SUBLANES:].astype(out_ref.dtype)


def filter_early_kernel(window_ref, halo_ref, samples_ref, out_ref):
    inputs, frames, nfft = samples_ref.shape
    unused = jnp.zeros((SUBLANES - (TAPS - 1), LANES), jnp.float32)
    for start in range(0, nfft, LANES):
        lanes = slice(start, start + LANES)
        window = [window_ref[tap : tap + 1, lanes] for tap in range(TAPS)]
        for a in range(inputs):
            halo = halo_ref[a, :, lanes].astype(jnp.float32)
            known = samples_ref[a, :, lanes].astype(jnp.float32)
            known = jnp.concatenate([unused, halo, known], axis=0)
            total = summed_taps(known, window)
            out_ref[a, :, lanes] = total[SUBLANES:].astype(out_ref.dtype)


def filter_late(window, samples):
    inputs, frames, nfft = samples.shape
    return pl.pallas_call(
        filter_late_kernel,
        grid=(inputs // BLOCK,),
        in_specs=[
            pl.BlockSpec(window.shape, lambda i: (0, 0)),
            pl.BlockSpec((BLOCK, frames, nfft), lambda i: (i, 0, 0)),
        ],
        out_specs=pl.BlockSpec((BLOCK, frames - EARLY, nfft), lambda i: (i, 0, 0)),
        out_shape=jax.ShapeDtypeStruct((inputs, frames - EARLY, nfft), jnp.bfloat16),
        compiler_params=pltpu.CompilerParams(
            dimension_semantics=("arbitrary",), vmem_limit_bytes=16 * MIB
        ),
        cost_estimate=pl.CostEstimate(
            flops=2 * TAPS * inputs * (frames - EARLY) * nfft,
            transcendentals=0,
            bytes_accessed=2 * inputs * (2 * frames - EARLY) * nfft,
        ),
        name="filter_late",
    )(window, samples)


def filter_early(window, halo, samples):
    inputs, frames, nfft = samples.shape
    return pl.pallas_call(
        filter_early_kernel,
        grid=(inputs // BLOCK,),
        in_specs=[
            pl.BlockSpec(window.shape, lambda i: (0, 0)),
            pl.BlockSpec((BLOCK, TAPS - 1, nfft), lambda i: (i, 0, 0)),
            pl.BlockSpec((BLOCK, EARLY, nfft), lambda i: (i, 0, 0)),
        ],
        out_specs=pl.BlockSpec((BLOCK, EARLY, nfft), lambda i: (i, 0, 0)),
        out_shape=jax.ShapeDtypeStruct((inputs, EARLY, nfft), jnp.bfloat16),
        compiler_params=pltpu.CompilerParams(
            dimension_semantics=("arbitrary",), vmem_limit_bytes=16 * MIB
        ),
        cost_estimate=pl.CostEstimate(
            flops=2 * TAPS * inputs * EARLY * nfft,
            transcendentals=0,
            bytes_accessed=4 * inputs * EARLY * nfft,
        ),
        name="filter_early",
    )(window, halo, samples)


def channelize_kernel(table_ref, gain_ref, early_ref, late_ref, out_ref, turned):
    inputs, _, nfft = late_ref.shape
    frames = early_ref.shape[1] + late_ref.shape[1]
    count = table_ref.shape[0] // 2
    table = table_ref[...]
    gain = jnp.transpose(gain_ref[...])
    lane = lax.broadcasted_iota(jnp.int32, (count, 2 * frames), 1)
    first = lane < frames
    for s in range(inputs // SUB):
        rows = []
        for a in range(s * SUB, (s + 1) * SUB):
            rows += [early_ref[a], late_ref[a]]
        both = lax.dot_general(
            table,
            jnp.concatenate(rows, axis=0),
            (((1,), (1,)), ((), ())),
            preferred_element_type=jnp.float32,
        )
        for j in range(SUB // 2):
            real = both[:count, j * 2 * frames : (j + 1) * 2 * frames]
            imag = both[count:, j * 2 * frames : (j + 1) * 2 * frames]
            even = jnp.where(first, real, pltpu.roll(imag, frames, 1))
            odd = jnp.where(first, pltpu.roll(real, frames, 1), imag)
            a = s * SUB + 2 * j
            turned[pl.ds(a, count, stride=PITCH), :] = even * gain[:, a : a + 1]
            turned[pl.ds(a + 1, count, stride=PITCH), :] = odd * gain[:, a + 1 : a + 2]
    spectra = turned[...].reshape(count, PITCH, 2 * frames)
    out_ref[...] = spectra[:, :inputs].astype(out_ref.dtype)


def channelize(table, gain, early, late):
    inputs, late_frames, nfft = late.shape
    frames = EARLY + late_frames
    count = table.shape[0] // 2
    return pl.pallas_call(
        channelize_kernel,
        grid=(inputs // BLOCK,),
        in_specs=[
            pl.BlockSpec(table.shape, lambda i: (0, 0)),
            pl.BlockSpec((BLOCK, count), lambda i: (i, 0)),
            pl.BlockSpec((BLOCK, EARLY, nfft), lambda i: (i, 0, 0)),
            pl.BlockSpec((BLOCK, late_frames, nfft), lambda i: (i, 0, 0)),
        ],
        out_specs=pl.BlockSpec((count, BLOCK, 2 * frames), lambda i: (0, i, 0)),
        out_shape=pltpu.HBM((count, inputs, 2 * frames), jnp.bfloat16),
        scratch_shapes=[pltpu.VMEM((count * PITCH, 2 * frames), jnp.float32)],
        compiler_params=pltpu.CompilerParams(
            dimension_semantics=("arbitrary",), vmem_limit_bytes=32 * MIB
        ),
        cost_estimate=pl.CostEstimate(
            flops=4 * count * inputs * frames * nfft,
            transcendentals=0,
            bytes_accessed=2 * (inputs * frames * nfft + count * inputs * 2 * frames),
        ),
        name="channelize",
    )(table, gain, early, late)


def correlate_kernel(frames_all, blocks_ref, out_ref):
    n_time = blocks_ref.shape[1]
    inputs_all = blocks_ref.shape[0] * blocks_ref.shape[3]
    width = blocks_ref.shape[4]
    half = width // 2
    straight, crossed = [], []
    for t in range(n_time):
        part = blocks_ref[:, t, 0].reshape(inputs_all, width)
        straight.append(part)
        crossed.append(jnp.concatenate([part[:, half:], -part[:, :half]], axis=1))
    straight = jnp.concatenate(straight, axis=1)
    crossed = jnp.concatenate(crossed, axis=1)
    last = (((1,), (1,)), ((), ()))
    scale = 1.0 / frames_all
    low, high = slice(0, inputs_all // 2), slice(inputs_all // 2, inputs_all)
    for rows, columns in ((low, low), (high, low), (high, high)):
        for k, left in enumerate((straight, crossed)):
            product = scale * lax.dot_general(
                left[rows], straight[columns], last, preferred_element_type=jnp.float32
            )
            out_ref[0, k, rows, columns] = product
            if rows != columns:
                mirrored = product.T
                out_ref[0, k, columns, rows] = mirrored if k == 0 else -mirrored


def correlate(arrived, frames_all):
    n_inp, n_time, chan_dev, local, width = arrived.shape
    inputs_all = n_inp * local
    return pl.pallas_call(
        functools.partial(correlate_kernel, frames_all),
        grid=(chan_dev,),
        in_specs=[pl.BlockSpec((n_inp, n_time, 1, local, width), lambda i: (0, 0, i, 0, 0))],
        out_specs=pl.BlockSpec((1, 2, inputs_all, inputs_all), lambda i: (i, 0, 0, 0)),
        out_shape=jax.ShapeDtypeStruct((chan_dev, 2, inputs_all, inputs_all), jnp.float32),
        compiler_params=pltpu.CompilerParams(
            dimension_semantics=("arbitrary",), vmem_limit_bytes=40 * MIB
        ),
        cost_estimate=pl.CostEstimate(
            flops=chan_dev * 3 * inputs_all * inputs_all * n_time * width,
            transcendentals=0,
            bytes_accessed=chan_dev
            * (2 * inputs_all * n_time * width + 8 * inputs_all * inputs_all),
        ),
        name="correlate",
    )(arrived)


def on_device(samples, eq_gain):
    local_inputs, local_frames, nfft = samples.shape
    channels = nfft // 2
    n_inp = lax.axis_size("inp")
    n_time = lax.axis_size("tm")
    groups = n_inp * n_time
    chan_dev = channels // groups
    frames_all = n_time * local_frames
    tail = samples[:, local_frames - (TAPS - 1) :, :]
    halo = passed_along(tail, "tm", 1)
    window = jnp.asarray(window_table(TAPS, nfft))
    table = jnp.asarray(fourier_table(channels, nfft))
    samples = pltpu.with_memory_space_constraint(samples, pltpu.HBM)
    late = filter_late(window, samples)
    early = filter_early(window, halo, samples)
    parcel = channelize(table, eq_gain.T, early, late)
    parcel = parcel.reshape(groups, chan_dev * local_inputs, 2 * local_frames)
    arrived = lax.all_to_all(parcel, ("inp", "tm"), split_axis=0, concat_axis=0, tiled=True)
    arrived = arrived.reshape(n_inp, n_time, chan_dev, local_inputs, 2 * local_frames)
    return correlate(arrived, frames_all)


def solution(mesh):
    placed = (P("inp", "tm", None), P(None, "inp"))
    return jax.shard_map(
        on_device,
        mesh=mesh,
        in_specs=placed,
        out_specs=P(("inp", "tm"), None, None, None),
        check_vma=False,
    )
```

```python
import functools
import math

import jax
import jax.numpy as jnp
import ml_dtypes
import numpy as np
from jax import lax
from jax.experimental import pallas as pl
from jax.experimental.pallas import tpu as pltpu
from jax.sharding import PartitionSpec as P

TAPS = 4
LANES = 128
SUBLANES = 8
BLOCK = 16
PAIRS = 8
SUB = 2
PITCH = 2 * PAIRS + 1
MIB = 2**20


def passed_along(array, axis, by):
    devices = lax.axis_size(axis)
    pairs = [(i, i + by) for i in range(devices) if 0 <= i + by < devices]
    return lax.ppermute(array, axis, pairs)


def window_table(taps, nfft):
    position = np.arange(taps * nfft, dtype=np.float64) + 0.5
    shape_part = np.sinc(position / nfft - taps / 2.0)
    taper = 0.5 - 0.5 * np.cos(position * (2.0 * math.pi / (taps * nfft)))
    return (shape_part * taper).reshape(taps, nfft).astype(np.float32)


def fourier_tables(channels, nfft):
    phase = (np.arange(channels)[:, None] * np.arange(nfft // 2)[None, :] % nfft) * (
        2.0 * math.pi / nfft
    )
    scale = 1.0 / math.sqrt(nfft)
    table = np.stack([np.cos(phase) * scale, -np.sin(phase) * scale])
    table = table.astype(np.float32).astype(ml_dtypes.bfloat16)
    table = table.reshape(2, channels // 2, 2, nfft // 2).transpose(2, 0, 1, 3)
    return table.reshape(2, channels, nfft // 2)


def summed_taps(frames, window_ref, lanes):
    window = [window_ref[tap : tap + 1, lanes] for tap in range(TAPS)]
    earlier = pltpu.roll(frames, 2, 0)
    odd = frames * window[2] + earlier * window[0]
    return frames * window[3] + earlier * window[1] + pltpu.roll(odd, 1, 0)


def folded(rows_of, window_ref, store, nfft):
    for start in range(0, nfft // 2, LANES):
        near = slice(start, start + LANES)
        far = slice(nfft // 2 + start, nfft // 2 + start + LANES)
        one = summed_taps(rows_of(near), window_ref, near)[SUBLANES:]
        two = summed_taps(rows_of(far), window_ref, far)[SUBLANES:]
        store(near, one + two)
        store(far, one - two)


def filter_late_kernel(window_ref, samples_ref, out_ref):
    inputs, frames, nfft = samples_ref.shape
    for a in range(inputs):

        def rows_of(lanes):
            return samples_ref[a, :, lanes].astype(jnp.float32)

        def store(lanes, rows):
            out_ref[a, SUBLANES:, lanes] = rows.astype(out_ref.dtype)

        folded(rows_of, window_ref, store, nfft)


def filter_early_kernel(window_ref, halo_ref, samples_ref, late_ref, out_ref):
    inputs, frames, nfft = samples_ref.shape
    unused = jnp.zeros((SUBLANES - (TAPS - 1), LANES), jnp.float32)
    for a in range(inputs):

        def rows_of(lanes):
            halo = halo_ref[a, :, lanes].astype(jnp.float32)
            known = samples_ref[a, :, lanes].astype(jnp.float32)
            return jnp.concatenate([unused, halo, known], axis=0)

        def store(lanes, rows):
            out_ref[a, :, lanes] = rows.astype(out_ref.dtype)

        folded(rows_of, window_ref, store, nfft)


def filter_late(window, samples):
    inputs, frames, nfft = samples.shape
    return pl.pallas_call(
        filter_late_kernel,
        grid=(inputs // BLOCK,),
        in_specs=[
            pl.BlockSpec(window.shape, lambda i: (0, 0)),
            pl.BlockSpec((BLOCK, frames, nfft), lambda i: (i, 0, 0)),
        ],
        out_specs=pl.BlockSpec((BLOCK, frames, nfft), lambda i: (i, 0, 0)),
        out_shape=jax.ShapeDtypeStruct((inputs, frames, nfft), jnp.bfloat16),
        compiler_params=pltpu.CompilerParams(
            dimension_semantics=("arbitrary",), vmem_limit_bytes=16 * MIB
        ),
        cost_estimate=pl.CostEstimate(
            flops=2 * TAPS * inputs * frames * nfft,
            transcendentals=0,
            bytes_accessed=4 * inputs * frames * nfft,
        ),
        name="filter_late",
    )(window, samples)


def filter_early(window, halo, samples, late):
    inputs, frames, nfft = samples.shape
    return pl.pallas_call(
        filter_early_kernel,
        grid=(inputs // BLOCK,),
        in_specs=[
            pl.BlockSpec(window.shape, lambda i: (0, 0)),
            pl.BlockSpec((BLOCK, TAPS - 1, nfft), lambda i: (i, 0, 0)),
            pl.BlockSpec((BLOCK, SUBLANES, nfft), lambda i: (i, 0, 0)),
            pl.BlockSpec(memory_space=pl.ANY),
        ],
        out_specs=pl.BlockSpec((BLOCK, SUBLANES, nfft), lambda i: (i, 0, 0)),
        out_shape=jax.ShapeDtypeStruct((inputs, frames, nfft), jnp.bfloat16),
        input_output_aliases={3: 0},
        compiler_params=pltpu.CompilerParams(
            dimension_semantics=("arbitrary",), vmem_limit_bytes=16 * MIB
        ),
        cost_estimate=pl.CostEstimate(
            flops=2 * TAPS * inputs * SUBLANES * nfft,
            transcendentals=0,
            bytes_accessed=4 * inputs * SUBLANES * nfft,
        ),
        name="filter_early",
    )(window, halo, samples, late)


def channelize_kernel(table_ref, gain_ref, rows_ref, out_ref, turned, gains):
    _, pairs, frames, nfft = rows_ref.shape
    depth = nfft // 2
    count = table_ref.shape[1] // 2
    lane = lax.broadcasted_iota(jnp.int32, (count, 2 * frames), 1)
    first = lane < frames
    unused = jnp.zeros((LANES - 2 * pairs, 2 * count), jnp.float32)
    gains[...] = jnp.transpose(jnp.concatenate([gain_ref[0], gain_ref[1], unused], axis=0))
    for parity in range(2):
        gain = gains[pl.ds(parity, count, stride=2), :]
        columns = slice(parity * depth, (parity + 1) * depth)
        for s in range(0, pairs, SUB):
            rows = [rows_ref[h, i, :, columns] for i in range(s, s + SUB) for h in range(2)]
            both = lax.dot_general(
                table_ref[parity],
                jnp.concatenate(rows, axis=0),
                (((1,), (1,)), ((), ())),
                preferred_element_type=jnp.float32,
            )
            for i in range(s, s + SUB):
                lanes = slice((i - s) * 2 * frames, (i - s + 1) * 2 * frames)
                scale = jnp.where(first, gain[:, i : i + 1], gain[:, pairs + i : pairs + i + 1])
                start = parity * count * PITCH + i
                turned[pl.ds(start, count, stride=PITCH), :] = both[:count, lanes] * scale
                turned[pl.ds(start + pairs, count, stride=PITCH), :] = both[count:, lanes] * scale
    for parity in range(2):
        for c in range(count):
            start = (parity * count + c) * PITCH
            for r in range(2):
                rows = turned[start + r * pairs : start + (r + 1) * pairs, :]
                out_ref[2 * c + parity, r] = rows.astype(out_ref.dtype)


def channelize(tables, gain, rows):
    inputs, frames, nfft = rows.shape
    channels = tables.shape[1]
    half = inputs // 2
    return pl.pallas_call(
        channelize_kernel,
        grid=(half // PAIRS,),
        in_specs=[
            pl.BlockSpec(tables.shape, lambda i: (0, 0, 0)),
            pl.BlockSpec((2, PAIRS, channels), lambda i: (0, i, 0)),
            pl.BlockSpec((2, PAIRS, frames, nfft), lambda i: (0, i, 0, 0)),
        ],
        out_specs=pl.BlockSpec((channels, 2, PAIRS, 2 * frames), lambda i: (0, 0, i, 0)),
        out_shape=pltpu.HBM((channels, 2, half, 2 * frames), jnp.bfloat16),
        scratch_shapes=[
            pltpu.VMEM((channels * PITCH, 2 * frames), jnp.float32),
            pltpu.VMEM((channels, LANES), jnp.float32),
        ],
        compiler_params=pltpu.CompilerParams(
            dimension_semantics=("arbitrary",), vmem_limit_bytes=32 * MIB
        ),
        cost_estimate=pl.CostEstimate(
            flops=2 * channels * inputs * frames * nfft,
            transcendentals=0,
            bytes_accessed=2 * (inputs * frames * nfft + channels * inputs * 2 * frames),
        ),
        name="channelize",
    )(tables, gain.reshape(2, half, channels), rows.reshape(2, half, frames, nfft))


def correlate_kernel(frames_all, blocks_ref, out_ref):
    n_time = blocks_ref.shape[1]
    inputs_all = blocks_ref.shape[0] * blocks_ref.shape[3]
    width = blocks_ref.shape[4]
    half = width // 2
    n_inp, pairs = blocks_ref.shape[0], blocks_ref.shape[3] // 2
    first = lax.broadcasted_iota(jnp.int32, (n_inp, pairs, width), 2) < half
    straight, crossed = [], []
    for t in range(n_time):
        real, imag = blocks_ref[:, t, 0, :pairs], blocks_ref[:, t, 0, pairs:]
        real_turned = jnp.concatenate([real[..., half:], real[..., :half]], axis=2)
        imag_turned = jnp.concatenate([imag[..., half:], imag[..., :half]], axis=2)
        low_rows = jnp.where(first, real, imag_turned)
        high_rows = jnp.where(first, real_turned, imag)
        rows = jnp.concatenate([low_rows, high_rows], axis=1)
        straight.append(rows.reshape(inputs_all, width))
        low_rows = jnp.where(first, imag, -real_turned)
        high_rows = jnp.where(first, imag_turned, -real)
        rows = jnp.concatenate([low_rows, high_rows], axis=1)
        crossed.append(rows.reshape(inputs_all, width))
    straight = jnp.concatenate(straight, axis=1)
    crossed = jnp.concatenate(crossed, axis=1)
    last = (((1,), (1,)), ((), ()))
    scale = 1.0 / frames_all
    low, high = slice(0, inputs_all // 2), slice(inputs_all // 2, inputs_all)
    for rows, columns in ((low, low), (high, low), (high, high)):
        for k, left in enumerate((straight, crossed)):
            product = scale * lax.dot_general(
                left[rows], straight[columns], last, preferred_element_type=jnp.float32
            )
            out_ref[0, k, rows, columns] = product
            if rows != columns:
                mirrored = product.T
                out_ref[0, k, columns, rows] = mirrored if k == 0 else -mirrored


def correlate(arrived, frames_all):
    n_inp, n_time, chan_dev, local, width = arrived.shape
    inputs_all = n_inp * local
    return pl.pallas_call(
        functools.partial(correlate_kernel, frames_all),
        grid=(chan_dev,),
        in_specs=[pl.BlockSpec((n_inp, n_time, 1, local, width), lambda i: (0, 0, i, 0, 0))],
        out_specs=pl.BlockSpec((1, 2, inputs_all, inputs_all), lambda i: (i, 0, 0, 0)),
        out_shape=jax.ShapeDtypeStruct((chan_dev, 2, inputs_all, inputs_all), jnp.float32),
        compiler_params=pltpu.CompilerParams(
            dimension_semantics=("arbitrary",), vmem_limit_bytes=40 * MIB
        ),
        cost_estimate=pl.CostEstimate(
            flops=chan_dev * 3 * inputs_all * inputs_all * n_time * width,
            transcendentals=0,
            bytes_accessed=chan_dev
            * (2 * inputs_all * n_time * width + 8 * inputs_all * inputs_all),
        ),
        name="correlate",
    )(arrived)


def on_device(samples, eq_gain):
    local_inputs, local_frames, nfft = samples.shape
    channels = nfft // 2
    n_inp = lax.axis_size("inp")
    n_time = lax.axis_size("tm")
    groups = n_inp * n_time
    chan_dev = channels // groups
    frames_all = n_time * local_frames
    tail = samples[:, local_frames - (TAPS - 1) :, :]
    halo = passed_along(tail, "tm", 1)
    window = jnp.asarray(window_table(TAPS, nfft))
    tables = jnp.asarray(fourier_tables(channels, nfft))
    samples = pltpu.with_memory_space_constraint(samples, pltpu.HBM)
    late = filter_late(window, samples)
    rows = filter_early(window, halo, samples, late)
    parcel = channelize(tables, eq_gain.T, rows)
    parcel = parcel.reshape(groups, chan_dev * local_inputs, 2 * local_frames)
    arrived = lax.all_to_all(parcel, ("inp", "tm"), split_axis=0, concat_axis=0, tiled=True)
    arrived = arrived.reshape(n_inp, n_time, chan_dev, local_inputs, 2 * local_frames)
    return correlate(arrived, frames_all)


def solution(mesh):
    placed = (P("inp", "tm", None), P(None, "inp"))
    return jax.shard_map(
        on_device,
        mesh=mesh,
        in_specs=placed,
        out_specs=P(("inp", "tm"), None, None, None),
        check_vma=False,
    )
```

```python
import functools
import math

import jax
import jax.numpy as jnp
import ml_dtypes
import numpy as np
from jax import lax
from jax.experimental import pallas as pl
from jax.experimental.pallas import tpu as pltpu
from jax.sharding import PartitionSpec as P

TAPS = 4
LANES = 128
SUBLANES = 8
BLOCK = 16
EARLY_BLOCK = 32
PAIRS = 8
SUB = 2
PITCH = 2 * PAIRS + 1
MIB = 2**20


def passed_along(array, axis, by):
    devices = lax.axis_size(axis)
    pairs = [(i, i + by) for i in range(devices) if 0 <= i + by < devices]
    return lax.ppermute(array, axis, pairs)


def window_table(taps, nfft):
    position = np.arange(taps * nfft, dtype=np.float64) + 0.5
    shape_part = np.sinc(position / nfft - taps / 2.0)
    taper = 0.5 - 0.5 * np.cos(position * (2.0 * math.pi / (taps * nfft)))
    return (shape_part * taper).reshape(taps, nfft).astype(np.float32)


def fourier_tables(channels, nfft):
    phase = (np.arange(channels)[:, None] * np.arange(nfft // 2)[None, :] % nfft) * (
        2.0 * math.pi / nfft
    )
    scale = 1.0 / math.sqrt(nfft)
    table = np.stack([np.cos(phase) * scale, -np.sin(phase) * scale])
    table = table.astype(np.float32).astype(ml_dtypes.bfloat16)
    table = table.reshape(2, channels // 2, 2, nfft // 2).transpose(2, 0, 1, 3)
    return table.reshape(2, channels, nfft // 2)


def summed_taps(frames, window_ref, lanes):
    window = [window_ref[tap : tap + 1, lanes] for tap in range(TAPS)]
    earlier = pltpu.roll(frames, 2, 0)
    odd = frames * window[2] + earlier * window[0]
    return frames * window[3] + earlier * window[1] + pltpu.roll(odd, 1, 0)


def folded(rows_of, window_ref, store, nfft):
    for start in range(0, nfft // 2, LANES):
        near = slice(start, start + LANES)
        far = slice(nfft // 2 + start, nfft // 2 + start + LANES)
        one = summed_taps(rows_of(near), window_ref, near)[SUBLANES:].astype(jnp.bfloat16)
        two = summed_taps(rows_of(far), window_ref, far)[SUBLANES:].astype(jnp.bfloat16)
        store(near, one + two)
        store(far, one - two)


def filter_late_kernel(window_ref, samples_ref, out_ref):
    inputs, frames, nfft = samples_ref.shape
    for a in range(inputs):

        def rows_of(lanes):
            return samples_ref[a, :, lanes].astype(jnp.float32)

        def store(lanes, rows):
            out_ref[a, SUBLANES:, lanes] = rows

        folded(rows_of, window_ref, store, nfft)


def filter_early_kernel(window_ref, halo_ref, samples_ref, late_ref, out_ref):
    inputs, frames, nfft = samples_ref.shape
    unused = jnp.zeros((SUBLANES - (TAPS - 1), LANES), jnp.float32)
    for a in range(inputs):

        def rows_of(lanes):
            halo = halo_ref[a, :, lanes].astype(jnp.float32)
            known = samples_ref[a, :, lanes].astype(jnp.float32)
            return jnp.concatenate([unused, halo, known], axis=0)

        def store(lanes, rows):
            out_ref[a, :, lanes] = rows

        folded(rows_of, window_ref, store, nfft)


def filter_late(window, samples):
    inputs, frames, nfft = samples.shape
    return pl.pallas_call(
        filter_late_kernel,
        grid=(inputs // BLOCK,),
        in_specs=[
            pl.BlockSpec(window.shape, lambda i: (0, 0)),
            pl.BlockSpec((BLOCK, frames, nfft), lambda i: (i, 0, 0)),
        ],
        out_specs=pl.BlockSpec((BLOCK, frames, nfft), lambda i: (i, 0, 0)),
        out_shape=jax.ShapeDtypeStruct((inputs, frames, nfft), jnp.bfloat16),
        compiler_params=pltpu.CompilerParams(
            dimension_semantics=("arbitrary",), vmem_limit_bytes=16 * MIB
        ),
        cost_estimate=pl.CostEstimate(
            flops=2 * TAPS * inputs * frames * nfft,
            transcendentals=0,
            bytes_accessed=4 * inputs * frames * nfft,
        ),
        name="filter_late",
    )(window, samples)


def filter_early(window, halo, samples, late):
    inputs, frames, nfft = samples.shape
    return pl.pallas_call(
        filter_early_kernel,
        grid=(inputs // EARLY_BLOCK,),
        in_specs=[
            pl.BlockSpec(window.shape, lambda i: (0, 0)),
            pl.BlockSpec((EARLY_BLOCK, TAPS - 1, nfft), lambda i: (i, 0, 0)),
            pl.BlockSpec((EARLY_BLOCK, SUBLANES, nfft), lambda i: (i, 0, 0)),
            pl.BlockSpec(memory_space=pl.ANY),
        ],
        out_specs=pl.BlockSpec((EARLY_BLOCK, SUBLANES, nfft), lambda i: (i, 0, 0)),
        out_shape=jax.ShapeDtypeStruct((inputs, frames, nfft), jnp.bfloat16),
        input_output_aliases={3: 0},
        compiler_params=pltpu.CompilerParams(
            dimension_semantics=("arbitrary",), vmem_limit_bytes=16 * MIB
        ),
        cost_estimate=pl.CostEstimate(
            flops=2 * TAPS * inputs * SUBLANES * nfft,
            transcendentals=0,
            bytes_accessed=4 * inputs * SUBLANES * nfft,
        ),
        name="filter_early",
    )(window, halo, samples, late)


def channelize_kernel(table_ref, gain_ref, rows_ref, out_ref, turned, gains):
    _, _, frames, nfft = rows_ref.shape
    pairs = PAIRS
    here = pl.program_id(0) * PAIRS
    depth = nfft // 2
    count = table_ref.shape[1] // 2
    lane = lax.broadcasted_iota(jnp.int32, (count, 2 * frames), 1)
    first = lane < frames
    unused = jnp.zeros((LANES - 2 * pairs, 2 * count), jnp.float32)
    gains[...] = jnp.transpose(jnp.concatenate([gain_ref[0], gain_ref[1], unused], axis=0))
    for parity in range(2):
        gain = gains[pl.ds(parity, count, stride=2), :]
        columns = slice(parity * depth, (parity + 1) * depth)
        for s in range(0, pairs, SUB):
            rows = [rows_ref[h, here + i, :, columns] for i in range(s, s + SUB) for h in range(2)]
            both = lax.dot_general(
                table_ref[parity],
                jnp.concatenate(rows, axis=0),
                (((1,), (1,)), ((), ())),
                preferred_element_type=jnp.float32,
            )
            for i in range(s, s + SUB):
                lanes = slice((i - s) * 2 * frames, (i - s + 1) * 2 * frames)
                scale = jnp.where(first, gain[:, i : i + 1], gain[:, pairs + i : pairs + i + 1])
                start = parity * count * PITCH + i
                turned[pl.ds(start, count, stride=PITCH), :] = both[:count, lanes] * scale
                turned[pl.ds(start + pairs, count, stride=PITCH), :] = both[count:, lanes] * scale
    for parity in range(2):
        for c in range(count):
            start = (parity * count + c) * PITCH
            for r in range(2):
                rows = turned[start + r * pairs : start + (r + 1) * pairs, :]
                out_ref[2 * c + parity, r] = rows.astype(out_ref.dtype)


def channelize(tables, gain, rows):
    inputs, frames, nfft = rows.shape
    channels = tables.shape[1]
    half = inputs // 2
    return pl.pallas_call(
        channelize_kernel,
        grid=(half // PAIRS,),
        in_specs=[
            pl.BlockSpec(tables.shape, lambda i: (0, 0, 0)),
            pl.BlockSpec((2, PAIRS, channels), lambda i: (0, i, 0)),
            pl.BlockSpec(memory_space=pltpu.VMEM),
        ],
        out_specs=pl.BlockSpec((channels, 2, PAIRS, 2 * frames), lambda i: (0, 0, i, 0)),
        out_shape=pltpu.HBM((channels, 2, half, 2 * frames), jnp.bfloat16),
        scratch_shapes=[
            pltpu.VMEM((channels * PITCH, 2 * frames), jnp.float32),
            pltpu.VMEM((channels, LANES), jnp.float32),
        ],
        compiler_params=pltpu.CompilerParams(
            dimension_semantics=("arbitrary",), vmem_limit_bytes=32 * MIB
        ),
        cost_estimate=pl.CostEstimate(
            flops=2 * channels * inputs * frames * nfft,
            transcendentals=0,
            bytes_accessed=2 * (inputs * frames * nfft + channels * inputs * 2 * frames),
        ),
        name="channelize",
    )(tables, gain.reshape(2, half, channels), rows.reshape(2, half, frames, nfft))


def correlate_kernel(frames_all, blocks_ref, out_ref):
    chan = pl.program_id(0)
    n_time = blocks_ref.shape[1]
    inputs_all = blocks_ref.shape[0] * blocks_ref.shape[3]
    width = blocks_ref.shape[4]
    half = width // 2
    n_inp, pairs = blocks_ref.shape[0], blocks_ref.shape[3] // 2
    first = lax.broadcasted_iota(jnp.int32, (n_inp, pairs, width), 2) < half
    straight, crossed = [], []
    for t in range(n_time):
        real, imag = blocks_ref[:, t, chan, :pairs], blocks_ref[:, t, chan, pairs:]
        real_turned = jnp.concatenate([real[..., half:], real[..., :half]], axis=2)
        imag_turned = jnp.concatenate([imag[..., half:], imag[..., :half]], axis=2)
        low_rows = jnp.where(first, real, imag_turned)
        high_rows = jnp.where(first, real_turned, imag)
        rows = jnp.concatenate([low_rows, high_rows], axis=1)
        straight.append(rows.reshape(inputs_all, width))
        low_rows = jnp.where(first, imag, -real_turned)
        high_rows = jnp.where(first, imag_turned, -real)
        rows = jnp.concatenate([low_rows, high_rows], axis=1)
        crossed.append(rows.reshape(inputs_all, width))
    straight = jnp.concatenate(straight, axis=1)
    crossed = jnp.concatenate(crossed, axis=1)
    last = (((1,), (1,)), ((), ()))
    scale = 1.0 / frames_all
    low, high = slice(0, inputs_all // 2), slice(inputs_all // 2, inputs_all)
    for rows, columns in ((low, low), (high, low), (high, high)):
        for k, left in enumerate((straight, crossed)):
            product = scale * lax.dot_general(
                left[rows], straight[columns], last, preferred_element_type=jnp.float32
            )
            out_ref[0, k, rows, columns] = product
            if rows != columns:
                mirrored = product.T
                out_ref[0, k, columns, rows] = mirrored if k == 0 else -mirrored


def correlate(arrived, frames_all):
    n_inp, n_time, chan_dev, local, width = arrived.shape
    inputs_all = n_inp * local
    return pl.pallas_call(
        functools.partial(correlate_kernel, frames_all),
        grid=(chan_dev,),
        in_specs=[pl.BlockSpec(memory_space=pltpu.VMEM)],
        out_specs=pl.BlockSpec((1, 2, inputs_all, inputs_all), lambda i: (i, 0, 0, 0)),
        out_shape=jax.ShapeDtypeStruct((chan_dev, 2, inputs_all, inputs_all), jnp.float32),
        compiler_params=pltpu.CompilerParams(
            dimension_semantics=("arbitrary",), vmem_limit_bytes=40 * MIB
        ),
        cost_estimate=pl.CostEstimate(
            flops=chan_dev * 3 * inputs_all * inputs_all * n_time * width,
            transcendentals=0,
            bytes_accessed=chan_dev
            * (2 * inputs_all * n_time * width + 8 * inputs_all * inputs_all),
        ),
        name="correlate",
    )(arrived)


def on_device(samples, eq_gain):
    local_inputs, local_frames, nfft = samples.shape
    channels = nfft // 2
    n_inp = lax.axis_size("inp")
    n_time = lax.axis_size("tm")
    groups = n_inp * n_time
    chan_dev = channels // groups
    frames_all = n_time * local_frames
    tail = samples[:, local_frames - (TAPS - 1) :, :]
    halo = passed_along(tail, "tm", 1)
    window = jnp.asarray(window_table(TAPS, nfft))
    window = pltpu.with_memory_space_constraint(window, pltpu.HBM)
    tables = jnp.asarray(fourier_tables(channels, nfft))
    samples = pltpu.with_memory_space_constraint(samples, pltpu.HBM)
    late = filter_late(window, samples)
    rows = filter_early(window, halo, samples, late)
    parcel = channelize(tables, eq_gain.T, rows)
    parcel = parcel.reshape(groups, chan_dev * local_inputs, 2 * local_frames)
    arrived = lax.all_to_all(parcel, ("inp", "tm"), split_axis=0, concat_axis=0, tiled=True)
    arrived = arrived.reshape(n_inp, n_time, chan_dev, local_inputs, 2 * local_frames)
    return correlate(arrived, frames_all)


def solution(mesh):
    placed = (P("inp", "tm", None), P(None, "inp"))
    return jax.shard_map(
        on_device,
        mesh=mesh,
        in_specs=placed,
        out_specs=P(("inp", "tm"), None, None, None),
        check_vma=False,
    )
```

```python
import functools
import math

import jax
import jax.numpy as jnp
import ml_dtypes
import numpy as np
from jax import lax
from jax.experimental import pallas as pl
from jax.experimental.pallas import tpu as pltpu
from jax.sharding import PartitionSpec as P

TAPS = 4
LANES = 128
SUBLANES = 8
BLOCK = 16
EARLY_BLOCK = 32
PAIRS = 8
SUB = 2
PITCH = 2 * PAIRS + 1
MIB = 2**20


def passed_along(array, axis, by):
    devices = lax.axis_size(axis)
    pairs = [(i, i + by) for i in range(devices) if 0 <= i + by < devices]
    return lax.ppermute(array, axis, pairs)


def window_table(taps, nfft):
    position = np.arange(taps * nfft, dtype=np.float64) + 0.5
    shape_part = np.sinc(position / nfft - taps / 2.0)
    taper = 0.5 - 0.5 * np.cos(position * (2.0 * math.pi / (taps * nfft)))
    return (shape_part * taper).reshape(taps, nfft).astype(np.float32)


def fourier_tables(channels, nfft):
    phase = (np.arange(channels)[:, None] * np.arange(nfft // 2)[None, :] % nfft) * (
        2.0 * math.pi / nfft
    )
    scale = 1.0 / math.sqrt(nfft)
    table = np.stack([np.cos(phase) * scale, -np.sin(phase) * scale])
    table = table.astype(np.float32).astype(ml_dtypes.bfloat16)
    table = table.reshape(2, channels // 2, 2, nfft // 2).transpose(2, 0, 1, 3)
    return table.reshape(2, channels, nfft // 2)


def summed_taps(frames, window):
    earlier = pltpu.roll(frames, 2, 0)
    odd = frames * window[2] + earlier * window[0]
    return frames * window[3] + earlier * window[1] + pltpu.roll(odd, 1, 0)


def folded(rows_of, window_ref, store, inputs, nfft):
    for start in range(0, nfft // 2, LANES):
        halves = [slice(at, at + LANES) for at in (start, nfft // 2 + start)]
        windows = [[window_ref[tap : tap + 1, h] for tap in range(TAPS)] for h in halves]
        for a in range(inputs):
            near, far = [
                summed_taps(rows_of(a, h), window)[SUBLANES:].astype(jnp.bfloat16)
                for h, window in zip(halves, windows)
            ]
            store(a, halves[0], near + far)
            store(a, halves[1], near - far)


def filter_late_kernel(window_ref, samples_ref, out_ref):
    inputs, frames, nfft = samples_ref.shape

    def rows_of(a, lanes):
        return samples_ref[a, :, lanes].astype(jnp.float32)

    def store(a, lanes, rows):
        out_ref[a, SUBLANES:, lanes] = rows

    folded(rows_of, window_ref, store, inputs, nfft)


def filter_early_kernel(window_ref, halo_ref, samples_ref, late_ref, out_ref):
    inputs, frames, nfft = samples_ref.shape
    unused = jnp.zeros((SUBLANES - (TAPS - 1), LANES), jnp.float32)

    def rows_of(a, lanes):
        halo = halo_ref[a, :, lanes].astype(jnp.float32)
        known = samples_ref[a, :, lanes].astype(jnp.float32)
        return jnp.concatenate([unused, halo, known], axis=0)

    def store(a, lanes, rows):
        out_ref[a, :, lanes] = rows

    folded(rows_of, window_ref, store, inputs, nfft)


def filter_late(window, samples):
    inputs, frames, nfft = samples.shape
    return pl.pallas_call(
        filter_late_kernel,
        grid=(inputs // BLOCK,),
        in_specs=[
            pl.BlockSpec(window.shape, lambda i: (0, 0)),
            pl.BlockSpec((BLOCK, frames, nfft), lambda i: (i, 0, 0)),
        ],
        out_specs=pl.BlockSpec((BLOCK, frames, nfft), lambda i: (i, 0, 0)),
        out_shape=jax.ShapeDtypeStruct((inputs, frames, nfft), jnp.bfloat16),
        compiler_params=pltpu.CompilerParams(
            dimension_semantics=("arbitrary",), vmem_limit_bytes=16 * MIB
        ),
        cost_estimate=pl.CostEstimate(
            flops=2 * TAPS * inputs * frames * nfft,
            transcendentals=0,
            bytes_accessed=4 * inputs * frames * nfft,
        ),
        name="filter_late",
    )(window, samples)


def filter_early(window, halo, samples, late):
    inputs, frames, nfft = samples.shape
    return pl.pallas_call(
        filter_early_kernel,
        grid=(inputs // EARLY_BLOCK,),
        in_specs=[
            pl.BlockSpec(window.shape, lambda i: (0, 0)),
            pl.BlockSpec((EARLY_BLOCK, TAPS - 1, nfft), lambda i: (i, 0, 0)),
            pl.BlockSpec((EARLY_BLOCK, SUBLANES, nfft), lambda i: (i, 0, 0)),
            pl.BlockSpec(memory_space=pl.ANY),
        ],
        out_specs=pl.BlockSpec((EARLY_BLOCK, SUBLANES, nfft), lambda i: (i, 0, 0)),
        out_shape=jax.ShapeDtypeStruct((inputs, frames, nfft), jnp.bfloat16),
        input_output_aliases={3: 0},
        compiler_params=pltpu.CompilerParams(
            dimension_semantics=("arbitrary",), vmem_limit_bytes=16 * MIB
        ),
        cost_estimate=pl.CostEstimate(
            flops=2 * TAPS * inputs * SUBLANES * nfft,
            transcendentals=0,
            bytes_accessed=4 * inputs * SUBLANES * nfft,
        ),
        name="filter_early",
    )(window, halo, samples, late)


def channelize_kernel(table_ref, gain_ref, rows_ref, out_ref, turned, gains):
    _, _, frames, nfft = rows_ref.shape
    pairs = PAIRS
    here = pl.program_id(0) * PAIRS
    depth = nfft // 2
    count = table_ref.shape[1] // 2
    lane = lax.broadcasted_iota(jnp.int32, (count, 2 * frames), 1)
    first = lane < frames
    unused = jnp.zeros((LANES - 2 * pairs, 2 * count), jnp.float32)
    gains[...] = jnp.transpose(jnp.concatenate([gain_ref[0], gain_ref[1], unused], axis=0))
    for parity in range(2):
        gain = gains[pl.ds(parity, count, stride=2), :]
        columns = slice(parity * depth, (parity + 1) * depth)
        for s in range(0, pairs, SUB):
            rows = [rows_ref[h, here + i, :, columns] for i in range(s, s + SUB) for h in range(2)]
            both = lax.dot_general(
                table_ref[parity],
                jnp.concatenate(rows, axis=0),
                (((1,), (1,)), ((), ())),
                preferred_element_type=jnp.float32,
            )
            for i in range(s, s + SUB):
                lanes = slice((i - s) * 2 * frames, (i - s + 1) * 2 * frames)
                scale = jnp.where(first, gain[:, i : i + 1], gain[:, pairs + i : pairs + i + 1])
                start = parity * count * PITCH + i
                turned[pl.ds(start, count, stride=PITCH), :] = both[:count, lanes] * scale
                turned[pl.ds(start + pairs, count, stride=PITCH), :] = both[count:, lanes] * scale
    for parity in range(2):
        for c in range(count):
            start = (parity * count + c) * PITCH
            for r in range(2):
                rows = turned[start + r * pairs : start + (r + 1) * pairs, :]
                out_ref[2 * c + parity, r] = rows.astype(out_ref.dtype)


def channelize(tables, gain, rows):
    inputs, frames, nfft = rows.shape
    channels = tables.shape[1]
    half = inputs // 2
    return pl.pallas_call(
        channelize_kernel,
        grid=(half // PAIRS,),
        in_specs=[
            pl.BlockSpec(tables.shape, lambda i: (0, 0, 0)),
            pl.BlockSpec((2, PAIRS, channels), lambda i: (0, i, 0)),
            pl.BlockSpec(memory_space=pltpu.VMEM),
        ],
        out_specs=pl.BlockSpec((channels, 2, PAIRS, 2 * frames), lambda i: (0, 0, i, 0)),
        out_shape=pltpu.HBM((channels, 2, half, 2 * frames), jnp.bfloat16),
        scratch_shapes=[
            pltpu.VMEM((channels * PITCH, 2 * frames), jnp.float32),
            pltpu.VMEM((channels, LANES), jnp.float32),
        ],
        compiler_params=pltpu.CompilerParams(
            dimension_semantics=("arbitrary",), vmem_limit_bytes=32 * MIB
        ),
        cost_estimate=pl.CostEstimate(
            flops=2 * channels * inputs * frames * nfft,
            transcendentals=0,
            bytes_accessed=2 * (inputs * frames * nfft + channels * inputs * 2 * frames),
        ),
        name="channelize",
    )(tables, gain.reshape(2, half, channels), rows.reshape(2, half, frames, nfft))


def correlate_kernel(frames_all, blocks_ref, out_ref):
    chan = pl.program_id(0)
    n_inp, n_time, _, local, width = blocks_ref.shape
    pairs, half = local // 2, width // 2
    inputs_all = n_inp * local
    first = lax.broadcasted_iota(jnp.int32, (n_inp, pairs, width), 2) < half
    parts = []
    for rows in (slice(0, pairs), slice(pairs, local)):
        columns = []
        for t in range(0, n_time, 2):
            one, two = blocks_ref[:, t, chan, rows], blocks_ref[:, t + 1, chan, rows]
            one_turned = jnp.concatenate([one[..., half:], one[..., :half]], axis=2)
            two_turned = jnp.concatenate([two[..., half:], two[..., :half]], axis=2)
            low_rows = jnp.where(first, one, two_turned)
            high_rows = jnp.where(first, one_turned, two)
            both = jnp.concatenate([low_rows, high_rows], axis=1)
            columns.append(both.reshape(inputs_all, width))
        parts.append(jnp.concatenate(columns, axis=1))
    real, imag = parts
    spectra = jnp.concatenate(parts, axis=1)
    last = (((1,), (1,)), ((), ()))
    scale = 1.0 / frames_all
    low, high = slice(0, inputs_all // 2), slice(inputs_all // 2, inputs_all)
    for rows, columns in ((low, low), (high, low), (high, high)):
        product = scale * lax.dot_general(
            spectra[rows], spectra[columns], last, preferred_element_type=jnp.float32
        )
        out_ref[0, 0, rows, columns] = product
        if rows != columns:
            out_ref[0, 0, columns, rows] = product.T
    product = scale * lax.dot_general(imag, real, last, preferred_element_type=jnp.float32)
    out_ref[0, 1] = product - product.T


def correlate(arrived, frames_all):
    n_inp, n_time, chan_dev, local, width = arrived.shape
    inputs_all = n_inp * local
    return pl.pallas_call(
        functools.partial(correlate_kernel, frames_all),
        grid=(chan_dev,),
        in_specs=[pl.BlockSpec(memory_space=pltpu.VMEM)],
        out_specs=pl.BlockSpec((1, 2, inputs_all, inputs_all), lambda i: (i, 0, 0, 0)),
        out_shape=jax.ShapeDtypeStruct((chan_dev, 2, inputs_all, inputs_all), jnp.float32),
        compiler_params=pltpu.CompilerParams(
            dimension_semantics=("arbitrary",), vmem_limit_bytes=40 * MIB
        ),
        cost_estimate=pl.CostEstimate(
            flops=chan_dev * 3 * inputs_all * inputs_all * n_time * width,
            transcendentals=0,
            bytes_accessed=chan_dev
            * (2 * inputs_all * n_time * width + 8 * inputs_all * inputs_all),
        ),
        name="correlate",
    )(arrived)


def on_device(samples, eq_gain):
    local_inputs, local_frames, nfft = samples.shape
    channels = nfft // 2
    n_inp = lax.axis_size("inp")
    n_time = lax.axis_size("tm")
    groups = n_inp * n_time
    chan_dev = channels // groups
    frames_all = n_time * local_frames
    tail = samples[:, local_frames - (TAPS - 1) :, :]
    halo = passed_along(tail, "tm", 1)
    window = jnp.asarray(window_table(TAPS, nfft))
    window = pltpu.with_memory_space_constraint(window, pltpu.HBM)
    tables = jnp.asarray(fourier_tables(channels, nfft))
    samples = pltpu.with_memory_space_constraint(samples, pltpu.HBM)
    late = filter_late(window, samples)
    rows = filter_early(window, halo, samples, late)
    parcel = channelize(tables, eq_gain.T, rows)
    parcel = parcel.reshape(groups, chan_dev * local_inputs, 2 * local_frames)
    arrived = lax.all_to_all(parcel, ("inp", "tm"), split_axis=0, concat_axis=0, tiled=True)
    arrived = arrived.reshape(n_inp, n_time, chan_dev, local_inputs, 2 * local_frames)
    return correlate(arrived, frames_all)


def solution(mesh):
    placed = (P("inp", "tm", None), P(None, "inp"))
    return jax.shard_map(
        on_device,
        mesh=mesh,
        in_specs=placed,
        out_specs=P(("inp", "tm"), None, None, None),
        check_vma=False,
    )
```

```python
import functools
import math

import jax
import jax.numpy as jnp
import ml_dtypes
import numpy as np
from jax import lax
from jax.experimental import pallas as pl
from jax.experimental.pallas import tpu as pltpu
from jax.sharding import PartitionSpec as P

TAPS = 4
LANES = 128
SUBLANES = 8
BLOCK = 16
EARLY_BLOCK = 32
PAIRS = 8
SUB = 2
PITCH = 2 * PAIRS + 1
MIB = 2**20


def passed_along(array, axis, by):
    devices = lax.axis_size(axis)
    pairs = [(i, i + by) for i in range(devices) if 0 <= i + by < devices]
    return lax.ppermute(array, axis, pairs)


def window_table(taps, nfft):
    position = np.arange(taps * nfft, dtype=np.float64) + 0.5
    shape_part = np.sinc(position / nfft - taps / 2.0)
    taper = 0.5 - 0.5 * np.cos(position * (2.0 * math.pi / (taps * nfft)))
    return (shape_part * taper).reshape(taps, nfft).astype(np.float32)


def fourier_tables(channels, nfft):
    phase = (np.arange(channels)[:, None] * np.arange(nfft // 2)[None, :] % nfft) * (
        2.0 * math.pi / nfft
    )
    scale = 1.0 / math.sqrt(nfft)
    table = np.stack([np.cos(phase) * scale, -np.sin(phase) * scale])
    table = table.astype(np.float32).astype(ml_dtypes.bfloat16)
    table = table.reshape(2, channels // 2, 2, nfft // 2).transpose(2, 0, 1, 3)
    return table.reshape(2, channels, nfft // 2)


def summed_taps(frames, window):
    earlier = pltpu.roll(frames, 2, 0)
    odd = frames * window[2] + earlier * window[0]
    return frames * window[3] + earlier * window[1] + pltpu.roll(odd, 1, 0)


def folded(rows_of, window_ref, store, inputs, nfft):
    for start in range(0, nfft // 2, LANES):
        halves = [slice(at, at + LANES) for at in (start, nfft // 2 + start)]
        windows = [[window_ref[tap : tap + 1, h] for tap in range(TAPS)] for h in halves]
        for a in range(inputs):
            near, far = [
                summed_taps(rows_of(a, h), window)[SUBLANES:].astype(jnp.bfloat16)
                for h, window in zip(halves, windows)
            ]
            store(a, halves[0], near + far)
            store(a, halves[1], near - far)


def filter_late_kernel(window_ref, samples_ref, out_ref):
    inputs, frames, nfft = samples_ref.shape

    def rows_of(a, lanes):
        return samples_ref[a, :, lanes].astype(jnp.float32)

    def store(a, lanes, rows):
        out_ref[a, SUBLANES:, lanes] = rows

    folded(rows_of, window_ref, store, inputs, nfft)


def filter_early_kernel(window_ref, halo_ref, samples_ref, late_ref, out_ref):
    inputs, frames, nfft = samples_ref.shape
    unused = jnp.zeros((SUBLANES - (TAPS - 1), LANES), jnp.float32)

    def rows_of(a, lanes):
        halo = halo_ref[a, :, lanes].astype(jnp.float32)
        known = samples_ref[a, :, lanes].astype(jnp.float32)
        return jnp.concatenate([unused, halo, known], axis=0)

    def store(a, lanes, rows):
        out_ref[a, :, lanes] = rows

    folded(rows_of, window_ref, store, inputs, nfft)


def filter_late(window, samples):
    inputs, frames, nfft = samples.shape
    return pl.pallas_call(
        filter_late_kernel,
        grid=(inputs // BLOCK,),
        in_specs=[
            pl.BlockSpec(window.shape, lambda i: (0, 0)),
            pl.BlockSpec((BLOCK, frames, nfft), lambda i: (i, 0, 0)),
        ],
        out_specs=pl.BlockSpec((BLOCK, frames, nfft), lambda i: (i, 0, 0)),
        out_shape=jax.ShapeDtypeStruct((inputs, frames, nfft), jnp.bfloat16),
        compiler_params=pltpu.CompilerParams(
            dimension_semantics=("arbitrary",), vmem_limit_bytes=16 * MIB
        ),
        cost_estimate=pl.CostEstimate(
            flops=2 * TAPS * inputs * frames * nfft,
            transcendentals=0,
            bytes_accessed=4 * inputs * frames * nfft,
        ),
        name="filter_late",
    )(window, samples)


def filter_early(window, halo, samples, late):
    inputs, frames, nfft = samples.shape
    return pl.pallas_call(
        filter_early_kernel,
        grid=(inputs // EARLY_BLOCK,),
        in_specs=[
            pl.BlockSpec(window.shape, lambda i: (0, 0)),
            pl.BlockSpec((EARLY_BLOCK, TAPS - 1, nfft), lambda i: (i, 0, 0)),
            pl.BlockSpec((EARLY_BLOCK, SUBLANES, nfft), lambda i: (i, 0, 0)),
            pl.BlockSpec(memory_space=pl.ANY),
        ],
        out_specs=pl.BlockSpec((EARLY_BLOCK, SUBLANES, nfft), lambda i: (i, 0, 0)),
        out_shape=jax.ShapeDtypeStruct((inputs, frames, nfft), jnp.bfloat16),
        input_output_aliases={3: 0},
        compiler_params=pltpu.CompilerParams(
            dimension_semantics=("arbitrary",), vmem_limit_bytes=16 * MIB
        ),
        cost_estimate=pl.CostEstimate(
            flops=2 * TAPS * inputs * SUBLANES * nfft,
            transcendentals=0,
            bytes_accessed=4 * inputs * SUBLANES * nfft,
        ),
        name="filter_early",
    )(window, halo, samples, late)


def channelize_kernel(table_ref, gain_ref, rows_ref, out_ref, turned, gains):
    _, _, frames, nfft = rows_ref.shape
    pairs = PAIRS
    here = pl.program_id(0) * PAIRS
    depth = nfft // 2
    count = table_ref.shape[1] // 2
    lane = lax.broadcasted_iota(jnp.int32, (count, 2 * frames), 1)
    first = lane < frames
    unused = jnp.zeros((LANES - 2 * pairs, 2 * count), jnp.float32)
    gains[...] = jnp.transpose(jnp.concatenate([gain_ref[0], gain_ref[1], unused], axis=0))
    for parity in range(2):
        gain = gains[pl.ds(parity, count, stride=2), :]
        columns = slice(parity * depth, (parity + 1) * depth)
        for s in range(0, pairs, SUB):
            rows = [rows_ref[h, here + i, :, columns] for i in range(s, s + SUB) for h in range(2)]
            both = lax.dot_general(
                table_ref[parity],
                jnp.concatenate(rows, axis=0),
                (((1,), (1,)), ((), ())),
                preferred_element_type=jnp.float32,
            )
            for i in range(s, s + SUB):
                lanes = slice((i - s) * 2 * frames, (i - s + 1) * 2 * frames)
                scale = jnp.where(first, gain[:, i : i + 1], gain[:, pairs + i : pairs + i + 1])
                start = parity * count * PITCH + i
                turned[pl.ds(start, count, stride=PITCH), :] = both[:count, lanes] * scale
                turned[pl.ds(start + pairs, count, stride=PITCH), :] = both[count:, lanes] * scale
    for parity in range(2):
        for c in range(count):
            start = (parity * count + c) * PITCH
            for r in range(2):
                rows = turned[start + r * pairs : start + (r + 1) * pairs, :]
                out_ref[2 * c + parity, r] = rows.astype(out_ref.dtype)


def channelize(tables, gain, rows):
    inputs, frames, nfft = rows.shape
    channels = tables.shape[1]
    half = inputs // 2
    return pl.pallas_call(
        channelize_kernel,
        grid=(half // PAIRS,),
        in_specs=[
            pl.BlockSpec(tables.shape, lambda i: (0, 0, 0)),
            pl.BlockSpec((2, PAIRS, channels), lambda i: (0, i, 0)),
            pl.BlockSpec(memory_space=pltpu.VMEM),
        ],
        out_specs=pl.BlockSpec((channels, 2, PAIRS, 2 * frames), lambda i: (0, 0, i, 0)),
        out_shape=jax.ShapeDtypeStruct((channels, 2, half, 2 * frames), jnp.bfloat16),
        scratch_shapes=[
            pltpu.VMEM((channels * PITCH, 2 * frames), jnp.float32),
            pltpu.VMEM((channels, LANES), jnp.float32),
        ],
        compiler_params=pltpu.CompilerParams(
            dimension_semantics=("arbitrary",), vmem_limit_bytes=32 * MIB
        ),
        cost_estimate=pl.CostEstimate(
            flops=2 * channels * inputs * frames * nfft,
            transcendentals=0,
            bytes_accessed=2 * (inputs * frames * nfft + channels * inputs * 2 * frames),
        ),
        name="channelize",
    )(tables, gain.reshape(2, half, channels), rows.reshape(2, half, frames, nfft))


def correlate_kernel(frames_all, blocks_ref, out_ref):
    chan = pl.program_id(0)
    n_inp, n_time, _, local, width = blocks_ref.shape
    pairs, half = local // 2, width // 2
    inputs_all = n_inp * local
    first = lax.broadcasted_iota(jnp.int32, (n_inp, pairs, width), 2) < half
    parts = []
    for rows in (slice(0, pairs), slice(pairs, local)):
        columns = []
        for t in range(0, n_time, 2):
            one, two = blocks_ref[:, t, chan, rows], blocks_ref[:, t + 1, chan, rows]
            one_turned = jnp.concatenate([one[..., half:], one[..., :half]], axis=2)
            two_turned = jnp.concatenate([two[..., half:], two[..., :half]], axis=2)
            low_rows = jnp.where(first, one, two_turned)
            high_rows = jnp.where(first, one_turned, two)
            both = jnp.concatenate([low_rows, high_rows], axis=1)
            columns.append(both.reshape(inputs_all, width))
        parts.append(jnp.concatenate(columns, axis=1))
    real, imag = parts
    spectra = jnp.concatenate(parts, axis=1)
    last = (((1,), (1,)), ((), ()))
    scale = 1.0 / frames_all
    low, high = slice(0, inputs_all // 2), slice(inputs_all // 2, inputs_all)
    for rows, columns in ((low, low), (high, low), (high, high)):
        product = scale * lax.dot_general(
            spectra[rows], spectra[columns], last, preferred_element_type=jnp.float32
        )
        out_ref[0, 0, rows, columns] = product
        if rows != columns:
            out_ref[0, 0, columns, rows] = product.T
    product = scale * lax.dot_general(imag, real, last, preferred_element_type=jnp.float32)
    out_ref[0, 1] = product - product.T


def correlate(arrived, frames_all):
    n_inp, n_time, chan_dev, local, width = arrived.shape
    inputs_all = n_inp * local
    return pl.pallas_call(
        functools.partial(correlate_kernel, frames_all),
        grid=(chan_dev,),
        in_specs=[pl.BlockSpec(memory_space=pltpu.VMEM)],
        out_specs=pl.BlockSpec((1, 2, inputs_all, inputs_all), lambda i: (i, 0, 0, 0)),
        out_shape=jax.ShapeDtypeStruct((chan_dev, 2, inputs_all, inputs_all), jnp.float32),
        compiler_params=pltpu.CompilerParams(
            dimension_semantics=("arbitrary",), vmem_limit_bytes=40 * MIB
        ),
        cost_estimate=pl.CostEstimate(
            flops=chan_dev * 3 * inputs_all * inputs_all * n_time * width,
            transcendentals=0,
            bytes_accessed=chan_dev
            * (2 * inputs_all * n_time * width + 8 * inputs_all * inputs_all),
        ),
        name="correlate",
    )(arrived)


def on_device(samples, eq_gain):
    local_inputs, local_frames, nfft = samples.shape
    channels = nfft // 2
    n_inp = lax.axis_size("inp")
    n_time = lax.axis_size("tm")
    groups = n_inp * n_time
    chan_dev = channels // groups
    frames_all = n_time * local_frames
    tail = samples[:, local_frames - (TAPS - 1) :, :]
    halo = passed_along(tail, "tm", 1)
    window = jnp.asarray(window_table(TAPS, nfft))
    window = pltpu.with_memory_space_constraint(window, pltpu.HBM)
    tables = jnp.asarray(fourier_tables(channels, nfft))
    samples = pltpu.with_memory_space_constraint(samples, pltpu.HBM)
    late = filter_late(window, samples)
    rows = filter_early(window, halo, samples, late)
    parcel = channelize(tables, eq_gain.T, rows)
    parcel = parcel.reshape(groups, chan_dev * local_inputs, 2 * local_frames)
    arrived = lax.all_to_all(parcel, ("inp", "tm"), split_axis=0, concat_axis=0, tiled=True)
    arrived = arrived.reshape(n_inp, n_time, chan_dev, local_inputs, 2 * local_frames)
    return correlate(arrived, frames_all)


def solution(mesh):
    placed = (P("inp", "tm", None), P(None, "inp"))
    return jax.shard_map(
        on_device,
        mesh=mesh,
        in_specs=placed,
        out_specs=P(("inp", "tm"), None, None, None),
        check_vma=False,
    )
```

```python
import functools
import math

import jax
import jax.numpy as jnp
import ml_dtypes
import numpy as np
from jax import lax
from jax.experimental import pallas as pl
from jax.experimental.pallas import tpu as pltpu
from jax.sharding import PartitionSpec as P

TAPS = 4
LANES = 128
SUBLANES = 8
BLOCK = 16
EARLY_BLOCK = 32
PAIRS = 8
SUB = 2
PITCH = 2 * PAIRS + 1
MIB = 2**20


def passed_along(array, axis, by):
    devices = lax.axis_size(axis)
    pairs = [(i, i + by) for i in range(devices) if 0 <= i + by < devices]
    return lax.ppermute(array, axis, pairs)


def window_table(taps, nfft):
    position = np.arange(taps * nfft, dtype=np.float64) + 0.5
    shape_part = np.sinc(position / nfft - taps / 2.0)
    taper = 0.5 - 0.5 * np.cos(position * (2.0 * math.pi / (taps * nfft)))
    return (shape_part * taper).reshape(taps, nfft).astype(np.float32)


def fourier_tables(channels, nfft):
    phase = (np.arange(channels)[:, None] * np.arange(nfft // 2)[None, :] % nfft) * (
        2.0 * math.pi / nfft
    )
    scale = 1.0 / math.sqrt(nfft)
    table = np.stack([np.cos(phase) * scale, -np.sin(phase) * scale])
    table = table.astype(np.float32).astype(ml_dtypes.bfloat16)
    table = table.reshape(2, channels // 2, 2, nfft // 2).transpose(2, 0, 1, 3)
    return table.reshape(2, channels, nfft // 2)


def summed_taps(frames, window):
    earlier = pltpu.roll(frames, 2, 0)
    odd = frames * window[2] + earlier * window[0]
    return frames * window[3] + earlier * window[1] + pltpu.roll(odd, 1, 0)


def folded(halo, samples, window_ref):
    nfft = samples.shape[1]
    unused = jnp.zeros((SUBLANES - (TAPS - 1), LANES), jnp.float32)
    sums, differences = [], []
    for start in range(0, nfft // 2, LANES):
        parts = []
        for at in (start, nfft // 2 + start):
            lanes = slice(at, at + LANES)
            window = [window_ref[tap : tap + 1, lanes] for tap in range(TAPS)]
            known = [unused, halo[:, lanes].astype(jnp.float32)]
            known.append(samples[:, lanes].astype(jnp.float32))
            total = summed_taps(jnp.concatenate(known, axis=0), window)
            parts.append(total[SUBLANES:].astype(jnp.bfloat16))
        sums.append(parts[0] + parts[1])
        differences.append(parts[0] - parts[1])
    return jnp.concatenate(sums, axis=1), jnp.concatenate(differences, axis=1)


def channelize_kernel(
    table_ref, gain_ref, window_ref, halo_ref, samples_ref, out_ref, turned, gains
):
    _, pairs, frames, _ = samples_ref.shape
    count = table_ref.shape[1] // 2
    lane = lax.broadcasted_iota(jnp.int32, (count, 2 * frames), 1)
    first = lane < frames
    unused = jnp.zeros((LANES - 2 * pairs, 2 * count), jnp.float32)
    gains[...] = jnp.transpose(jnp.concatenate([gain_ref[0], gain_ref[1], unused], axis=0))
    gain_of = [gains[pl.ds(parity, count, stride=2), :] for parity in range(2)]
    for s in range(0, pairs, SUB):
        filtered = [
            folded(halo_ref[h, i], samples_ref[h, i], window_ref)
            for i in range(s, s + SUB)
            for h in range(2)
        ]
        for parity in range(2):
            gain = gain_of[parity]
            both = lax.dot_general(
                table_ref[parity],
                jnp.concatenate([rows[parity] for rows in filtered], axis=0),
                (((1,), (1,)), ((), ())),
                preferred_element_type=jnp.float32,
            )
            for i in range(s, s + SUB):
                lanes = slice((i - s) * 2 * frames, (i - s + 1) * 2 * frames)
                scale = jnp.where(first, gain[:, i : i + 1], gain[:, pairs + i : pairs + i + 1])
                start = parity * count * PITCH + i
                turned[pl.ds(start, count, stride=PITCH), :] = both[:count, lanes] * scale
                turned[pl.ds(start + pairs, count, stride=PITCH), :] = both[count:, lanes] * scale
    for parity in range(2):
        for c in range(count):
            start = (parity * count + c) * PITCH
            for r in range(2):
                rows = turned[start + r * pairs : start + (r + 1) * pairs, :]
                out_ref[2 * c + parity, r] = rows.astype(out_ref.dtype)


def channelize(tables, gain, window, halo, samples):
    inputs, frames, nfft = samples.shape
    channels = tables.shape[1]
    half = inputs // 2
    return pl.pallas_call(
        channelize_kernel,
        grid=(half // PAIRS,),
        in_specs=[
            pl.BlockSpec(tables.shape, lambda i: (0, 0, 0)),
            pl.BlockSpec((2, PAIRS, channels), lambda i: (0, i, 0)),
            pl.BlockSpec(window.shape, lambda i: (0, 0)),
            pl.BlockSpec((2, PAIRS, TAPS - 1, nfft), lambda i: (0, i, 0, 0)),
            pl.BlockSpec((2, PAIRS, frames, nfft), lambda i: (0, i, 0, 0)),
        ],
        out_specs=pl.BlockSpec((channels, 2, PAIRS, 2 * frames), lambda i: (0, 0, i, 0)),
        out_shape=pltpu.HBM((channels, 2, half, 2 * frames), jnp.bfloat16),
        scratch_shapes=[
            pltpu.VMEM((channels * PITCH, 2 * frames), jnp.float32),
            pltpu.VMEM((channels, LANES), jnp.float32),
        ],
        compiler_params=pltpu.CompilerParams(
            dimension_semantics=("arbitrary",), vmem_limit_bytes=32 * MIB
        ),
        cost_estimate=pl.CostEstimate(
            flops=2 * channels * inputs * frames * nfft,
            transcendentals=0,
            bytes_accessed=2 * (inputs * frames * nfft + channels * inputs * 2 * frames),
        ),
        name="channelize",
    )(
        tables,
        gain.reshape(2, half, channels),
        window,
        halo.reshape(2, half, TAPS - 1, nfft),
        pltpu.with_memory_space_constraint(
            samples.reshape(2, half, frames, nfft), pltpu.HBM
        ),
    )


def correlate_kernel(frames_all, blocks_ref, out_ref):
    chan = pl.program_id(0)
    n_inp, n_time, _, local, width = blocks_ref.shape
    pairs, half = local // 2, width // 2
    inputs_all = n_inp * local
    first = lax.broadcasted_iota(jnp.int32, (n_inp, pairs, width), 2) < half
    parts = []
    for rows in (slice(0, pairs), slice(pairs, local)):
        columns = []
        for t in range(0, n_time, 2):
            one, two = blocks_ref[:, t, chan, rows], blocks_ref[:, t + 1, chan, rows]
            one_turned = jnp.concatenate([one[..., half:], one[..., :half]], axis=2)
            two_turned = jnp.concatenate([two[..., half:], two[..., :half]], axis=2)
            low_rows = jnp.where(first, one, two_turned)
            high_rows = jnp.where(first, one_turned, two)
            both = jnp.concatenate([low_rows, high_rows], axis=1)
            columns.append(both.reshape(inputs_all, width))
        parts.append(jnp.concatenate(columns, axis=1))
    real, imag = parts
    spectra = jnp.concatenate(parts, axis=1)
    last = (((1,), (1,)), ((), ()))
    scale = 1.0 / frames_all
    low, high = slice(0, inputs_all // 2), slice(inputs_all // 2, inputs_all)
    for rows, columns in ((low, low), (high, low), (high, high)):
        product = scale * lax.dot_general(
            spectra[rows], spectra[columns], last, preferred_element_type=jnp.float32
        )
        out_ref[0, 0, rows, columns] = product
        if rows != columns:
            out_ref[0, 0, columns, rows] = product.T
    product = scale * lax.dot_general(imag, real, last, preferred_element_type=jnp.float32)
    out_ref[0, 1] = product - product.T


def correlate(arrived, frames_all):
    n_inp, n_time, chan_dev, local, width = arrived.shape
    inputs_all = n_inp * local
    return pl.pallas_call(
        functools.partial(correlate_kernel, frames_all),
        grid=(chan_dev,),
        in_specs=[pl.BlockSpec(memory_space=pltpu.VMEM)],
        out_specs=pl.BlockSpec((1, 2, inputs_all, inputs_all), lambda i: (i, 0, 0, 0)),
        out_shape=jax.ShapeDtypeStruct((chan_dev, 2, inputs_all, inputs_all), jnp.float32),
        compiler_params=pltpu.CompilerParams(
            dimension_semantics=("arbitrary",), vmem_limit_bytes=40 * MIB
        ),
        cost_estimate=pl.CostEstimate(
            flops=chan_dev * 3 * inputs_all * inputs_all * n_time * width,
            transcendentals=0,
            bytes_accessed=chan_dev
            * (2 * inputs_all * n_time * width + 8 * inputs_all * inputs_all),
        ),
        name="correlate",
    )(arrived)


def on_device(samples, eq_gain):
    local_inputs, local_frames, nfft = samples.shape
    channels = nfft // 2
    n_inp = lax.axis_size("inp")
    n_time = lax.axis_size("tm")
    groups = n_inp * n_time
    chan_dev = channels // groups
    frames_all = n_time * local_frames
    tail = samples[:, local_frames - (TAPS - 1) :, :]
    halo = passed_along(tail, "tm", 1)
    window = jnp.asarray(window_table(TAPS, nfft))
    window = pltpu.with_memory_space_constraint(window, pltpu.HBM)
    tables = jnp.asarray(fourier_tables(channels, nfft))
    parcel = channelize(tables, eq_gain.T, window, halo, samples)
    parcel = parcel.reshape(groups, chan_dev * local_inputs, 2 * local_frames)
    arrived = lax.all_to_all(parcel, ("inp", "tm"), split_axis=0, concat_axis=0, tiled=True)
    arrived = arrived.reshape(n_inp, n_time, chan_dev, local_inputs, 2 * local_frames)
    return correlate(arrived, frames_all)


def solution(mesh):
    placed = (P("inp", "tm", None), P(None, "inp"))
    return jax.shard_map(
        on_device,
        mesh=mesh,
        in_specs=placed,
        out_specs=P(("inp", "tm"), None, None, None),
        check_vma=False,
    )
```

```python
import functools
import math

import jax
import jax.numpy as jnp
import ml_dtypes
import numpy as np
from jax import lax
from jax.experimental import pallas as pl
from jax.experimental.pallas import tpu as pltpu
from jax.sharding import PartitionSpec as P

TAPS = 4
LANES = 128
SUBLANES = 8
BLOCK = 8
EARLY_BLOCK = 32
PAIRS = 8
SUB = 2
PITCH = 2 * PAIRS + 1
MIB = 2**20


def passed_along(array, axis, by):
    devices = lax.axis_size(axis)
    pairs = [(i, i + by) for i in range(devices) if 0 <= i + by < devices]
    return lax.ppermute(array, axis, pairs)


def window_table(taps, nfft):
    position = np.arange(taps * nfft, dtype=np.float64) + 0.5
    shape_part = np.sinc(position / nfft - taps / 2.0)
    taper = 0.5 - 0.5 * np.cos(position * (2.0 * math.pi / (taps * nfft)))
    return (shape_part * taper).reshape(taps, nfft).astype(np.float32)


def fourier_tables(channels, nfft):
    phase = (np.arange(channels)[:, None] * np.arange(nfft // 2)[None, :] % nfft) * (
        2.0 * math.pi / nfft
    )
    scale = 1.0 / math.sqrt(nfft)
    table = np.stack([np.cos(phase) * scale, -np.sin(phase) * scale])
    table = table.astype(np.float32).astype(ml_dtypes.bfloat16)
    table = table.reshape(2, channels // 2, 2, nfft // 2).transpose(2, 0, 1, 3)
    return table.reshape(2, channels, nfft // 2)


def summed_taps(frames, window):
    earlier = pltpu.roll(frames, 2, 0)
    odd = frames * window[2] + earlier * window[0]
    return frames * window[3] + earlier * window[1] + pltpu.roll(odd, 1, 0)


def folded(rows_of, window_ref, store, inputs, nfft):
    for start in range(0, nfft // 2, LANES):
        halves = [slice(at, at + LANES) for at in (start, nfft // 2 + start)]
        windows = [[window_ref[tap : tap + 1, h] for tap in range(TAPS)] for h in halves]
        for a in range(inputs):
            near, far = [
                summed_taps(rows_of(a, h), window)[SUBLANES:].astype(jnp.bfloat16)
                for h, window in zip(halves, windows)
            ]
            store(a, halves[0], near + far)
            store(a, halves[1], near - far)


def filter_late_kernel(taps_ref, samples_ref, out_ref, window_ref, held, ready, arrived):
    inputs, frames, nfft = samples_ref.shape

    def copy(k):
        some = pl.ds(k * BLOCK, BLOCK)
        return pltpu.make_async_copy(samples_ref.at[some], held.at[some], arrived.at[k])

    taps = pltpu.make_async_copy(taps_ref, window_ref, ready)
    taps.start()
    for k in range(inputs // BLOCK):
        copy(k).start()
    taps.wait()

    def step(k, carry):
        copy(k).wait()

        def rows_of(a, lanes):
            return held[k * BLOCK + a, :, lanes].astype(jnp.float32)

        def store(a, lanes, rows):
            out_ref[k * BLOCK + a, SUBLANES:, lanes] = rows

        folded(rows_of, window_ref, store, BLOCK, nfft)
        return carry

    lax.fori_loop(0, inputs // BLOCK, step, 0)


def filter_early_kernel(window_ref, halo_ref, samples_ref, late_ref, out_ref):
    inputs, frames, nfft = samples_ref.shape
    unused = jnp.zeros((SUBLANES - (TAPS - 1), LANES), jnp.float32)

    def rows_of(a, lanes):
        halo = halo_ref[a, :, lanes].astype(jnp.float32)
        known = samples_ref[a, :, lanes].astype(jnp.float32)
        return jnp.concatenate([unused, halo, known], axis=0)

    def store(a, lanes, rows):
        out_ref[a, :, lanes] = rows

    folded(rows_of, window_ref, store, inputs, nfft)


def filter_late(window, samples):
    inputs, frames, nfft = samples.shape
    return pl.pallas_call(
        filter_late_kernel,
        in_specs=[
            pl.BlockSpec(memory_space=pl.ANY),
            pl.BlockSpec(memory_space=pl.ANY),
        ],
        out_specs=pl.BlockSpec(memory_space=pltpu.VMEM),
        out_shape=jax.ShapeDtypeStruct((inputs, frames, nfft), jnp.bfloat16),
        scratch_shapes=[
            pltpu.VMEM(window.shape, window.dtype),
            pltpu.VMEM(samples.shape, samples.dtype),
            pltpu.SemaphoreType.DMA,
            pltpu.SemaphoreType.DMA((inputs // BLOCK,)),
        ],
        compiler_params=pltpu.CompilerParams(vmem_limit_bytes=16 * MIB),
        cost_estimate=pl.CostEstimate(
            flops=2 * TAPS * inputs * frames * nfft,
            transcendentals=0,
            bytes_accessed=4 * inputs * frames * nfft,
        ),
        name="filter_late",
    )(window, samples)


def filter_early(window, halo, samples, late):
    inputs, frames, nfft = samples.shape
    return pl.pallas_call(
        filter_early_kernel,
        grid=(inputs // EARLY_BLOCK,),
        in_specs=[
            pl.BlockSpec(window.shape, lambda i: (0, 0)),
            pl.BlockSpec((EARLY_BLOCK, TAPS - 1, nfft), lambda i: (i, 0, 0)),
            pl.BlockSpec((EARLY_BLOCK, SUBLANES, nfft), lambda i: (i, 0, 0)),
            pl.BlockSpec(memory_space=pl.ANY),
        ],
        out_specs=pl.BlockSpec((EARLY_BLOCK, SUBLANES, nfft), lambda i: (i, 0, 0)),
        out_shape=jax.ShapeDtypeStruct((inputs, frames, nfft), jnp.bfloat16),
        input_output_aliases={3: 0},
        compiler_params=pltpu.CompilerParams(
            dimension_semantics=("arbitrary",), vmem_limit_bytes=16 * MIB
        ),
        cost_estimate=pl.CostEstimate(
            flops=2 * TAPS * inputs * SUBLANES * nfft,
            transcendentals=0,
            bytes_accessed=4 * inputs * SUBLANES * nfft,
        ),
        name="filter_early",
    )(window, halo, samples, late)


def channelize_kernel(table_ref, gain_ref, rows_ref, out_ref, turned, gains):
    _, _, frames, nfft = rows_ref.shape
    pairs = PAIRS
    here = pl.program_id(0) * PAIRS
    depth = nfft // 2
    count = table_ref.shape[1] // 2
    lane = lax.broadcasted_iota(jnp.int32, (count, 2 * frames), 1)
    first = lane < frames
    unused = jnp.zeros((LANES - 2 * pairs, 2 * count), jnp.float32)
    gains[...] = jnp.transpose(jnp.concatenate([gain_ref[0], gain_ref[1], unused], axis=0))
    for parity in range(2):
        gain = gains[pl.ds(parity, count, stride=2), :]
        columns = slice(parity * depth, (parity + 1) * depth)
        for s in range(0, pairs, SUB):
            rows = [rows_ref[h, here + i, :, columns] for i in range(s, s + SUB) for h in range(2)]
            both = lax.dot_general(
                table_ref[parity],
                jnp.concatenate(rows, axis=0),
                (((1,), (1,)), ((), ())),
                preferred_element_type=jnp.float32,
            )
            for i in range(s, s + SUB):
                lanes = slice((i - s) * 2 * frames, (i - s + 1) * 2 * frames)
                scale = jnp.where(first, gain[:, i : i + 1], gain[:, pairs + i : pairs + i + 1])
                start = parity * count * PITCH + i
                turned[pl.ds(start, count, stride=PITCH), :] = both[:count, lanes] * scale
                turned[pl.ds(start + pairs, count, stride=PITCH), :] = both[count:, lanes] * scale
    for parity in range(2):
        for c in range(count):
            start = (parity * count + c) * PITCH
            for r in range(2):
                rows = turned[start + r * pairs : start + (r + 1) * pairs, :]
                out_ref[2 * c + parity, r] = rows.astype(out_ref.dtype)


def channelize(tables, gain, rows):
    inputs, frames, nfft = rows.shape
    channels = tables.shape[1]
    half = inputs // 2
    return pl.pallas_call(
        channelize_kernel,
        grid=(half // PAIRS,),
        in_specs=[
            pl.BlockSpec(tables.shape, lambda i: (0, 0, 0)),
            pl.BlockSpec((2, PAIRS, channels), lambda i: (0, i, 0)),
            pl.BlockSpec(memory_space=pltpu.VMEM),
        ],
        out_specs=pl.BlockSpec((channels, 2, PAIRS, 2 * frames), lambda i: (0, 0, i, 0)),
        out_shape=jax.ShapeDtypeStruct((channels, 2, half, 2 * frames), jnp.bfloat16),
        scratch_shapes=[
            pltpu.VMEM((channels * PITCH, 2 * frames), jnp.float32),
            pltpu.VMEM((channels, LANES), jnp.float32),
        ],
        compiler_params=pltpu.CompilerParams(
            dimension_semantics=("arbitrary",), vmem_limit_bytes=32 * MIB
        ),
        cost_estimate=pl.CostEstimate(
            flops=2 * channels * inputs * frames * nfft,
            transcendentals=0,
            bytes_accessed=2 * (inputs * frames * nfft + channels * inputs * 2 * frames),
        ),
        name="channelize",
    )(tables, gain.reshape(2, half, channels), rows.reshape(2, half, frames, nfft))


def correlate_kernel(frames_all, blocks_ref, out_ref):
    chan = pl.program_id(0)
    n_inp, n_time, _, local, width = blocks_ref.shape
    pairs, half = local // 2, width // 2
    inputs_all = n_inp * local
    first = lax.broadcasted_iota(jnp.int32, (n_inp, pairs, width), 2) < half
    parts = []
    for rows in (slice(0, pairs), slice(pairs, local)):
        columns = []
        for t in range(0, n_time, 2):
            one, two = blocks_ref[:, t, chan, rows], blocks_ref[:, t + 1, chan, rows]
            one_turned = jnp.concatenate([one[..., half:], one[..., :half]], axis=2)
            two_turned = jnp.concatenate([two[..., half:], two[..., :half]], axis=2)
            low_rows = jnp.where(first, one, two_turned)
            high_rows = jnp.where(first, one_turned, two)
            both = jnp.concatenate([low_rows, high_rows], axis=1)
            columns.append(both.reshape(inputs_all, width))
        parts.append(jnp.concatenate(columns, axis=1))
    real, imag = parts
    spectra = jnp.concatenate(parts, axis=1)
    last = (((1,), (1,)), ((), ()))
    scale = 1.0 / frames_all
    low, high = slice(0, inputs_all // 2), slice(inputs_all // 2, inputs_all)
    for rows, columns in ((low, low), (high, low), (high, high)):
        product = scale * lax.dot_general(
            spectra[rows], spectra[columns], last, preferred_element_type=jnp.float32
        )
        out_ref[0, 0, rows, columns] = product
        if rows != columns:
            out_ref[0, 0, columns, rows] = product.T
    product = scale * lax.dot_general(imag, real, last, preferred_element_type=jnp.float32)
    out_ref[0, 1] = product - product.T


def correlate(arrived, frames_all):
    n_inp, n_time, chan_dev, local, width = arrived.shape
    inputs_all = n_inp * local
    return pl.pallas_call(
        functools.partial(correlate_kernel, frames_all),
        grid=(chan_dev,),
        in_specs=[pl.BlockSpec(memory_space=pltpu.VMEM)],
        out_specs=pl.BlockSpec((1, 2, inputs_all, inputs_all), lambda i: (i, 0, 0, 0)),
        out_shape=jax.ShapeDtypeStruct((chan_dev, 2, inputs_all, inputs_all), jnp.float32),
        compiler_params=pltpu.CompilerParams(
            dimension_semantics=("arbitrary",), vmem_limit_bytes=40 * MIB
        ),
        cost_estimate=pl.CostEstimate(
            flops=chan_dev * 3 * inputs_all * inputs_all * n_time * width,
            transcendentals=0,
            bytes_accessed=chan_dev
            * (2 * inputs_all * n_time * width + 8 * inputs_all * inputs_all),
        ),
        name="correlate",
    )(arrived)


def on_device(samples, eq_gain):
    local_inputs, local_frames, nfft = samples.shape
    channels = nfft // 2
    n_inp = lax.axis_size("inp")
    n_time = lax.axis_size("tm")
    groups = n_inp * n_time
    chan_dev = channels // groups
    frames_all = n_time * local_frames
    tail = samples[:, local_frames - (TAPS - 1) :, :]
    halo = passed_along(tail, "tm", 1)
    window = jnp.asarray(window_table(TAPS, nfft))
    window = pltpu.with_memory_space_constraint(window, pltpu.HBM)
    tables = jnp.asarray(fourier_tables(channels, nfft))
    samples = pltpu.with_memory_space_constraint(samples, pltpu.HBM)
    late = filter_late(window, samples)
    rows = filter_early(window, halo, samples, late)
    parcel = channelize(tables, eq_gain.T, rows)
    parcel = parcel.reshape(groups, chan_dev * local_inputs, 2 * local_frames)
    arrived = lax.all_to_all(parcel, ("inp", "tm"), split_axis=0, concat_axis=0, tiled=True)
    arrived = arrived.reshape(n_inp, n_time, chan_dev, local_inputs, 2 * local_frames)
    return correlate(arrived, frames_all)


def solution(mesh):
    placed = (P("inp", "tm", None), P(None, "inp"))
    return jax.shard_map(
        on_device,
        mesh=mesh,
        in_specs=placed,
        out_specs=P(("inp", "tm"), None, None, None),
        check_vma=False,
    )
```
